32 devices in a mesh: wide: 8 (over z, y), narrow: 4 (over x, core).
Axes of the slice: x: 2, y: 2, z: 4, core: 2. Of those that a mesh axis runs over, the one named last changes fastest.
Arguments:
- right_side: float32 [112, 224, 256], P('narrow', 'wide'), may hold values from -60 to 60
- initial_guess: float32 [112, 224, 256], P('narrow', 'wide'), may hold values from -6 to 6
- class_map: int32 [112, 224], P('narrow', 'wide'), may hold values from 0 to 7
- class_conductivity: float32 [8], replicated, may hold values from 0.2 to 2
- window_index: int32 [4, 8, 1024], P('narrow', 'wide'), may hold values from 0 to 1023, each once within a row
- local_inverse: float32 [4, 8, 1024, 1024], P('narrow', 'wide'), may hold values from -1 to 1
- coarse_basis: float32 [4, 8, 4, 1024], P('narrow', 'wide'), may hold values from -0.1875 to 0.1875
- coarse_inverse: float32 [128, 128], P('wide', 'narrow'), may hold values from -8 to 8
Outputs:
- solution: float32 [112, 224, 256], P('narrow', 'wide')
- residual: float32 [112, 224, 256], P('narrow', 'wide')
The draws below stay inside these ranges and needn't reach their ends.
All inputs are finite; a program needn't handle non-finite values.
Results may differ from the reference program's by a relative error of at most 0.00013.
Values sent between devices are 32-bit elements; how exact they have to be, the bound alone decides.
A program may use at most 64 MiB of HBM per device.

```python
import math
import jax
import jax.numpy as jnp
from jax import lax

ES = 32
OV = 2
MODES = 4
ITERS = 3
CLASSES = 8
NRHS = 256
CS = 28
LOCAL = 1024
SROWS = 4
SCOLS = 8
NX = 112
NY = 224
NC = 128


def draw_right_side(key, part):
    key_noise = jax.random.fold_in(key, 11)
    col_pos = jnp.arange(NY, dtype=jnp.float32)[None, :, None]
    across = jnp.exp(math.log(10.0) * col_pos / (NY - 1))
    sample = jax.random.truncated_normal(key_noise, -6.0, 6.0, (NX, NY, NRHS), jnp.float32)
    return sample * across


def draw_local_inverse(key, part):
    key_off = jax.random.fold_in(key, 23)
    shape_full = (SROWS, SCOLS, LOCAL, LOCAL)
    identity = jnp.eye(LOCAL, dtype=jnp.float32)
    sample = jax.random.truncated_normal(key_off, -6.0, 6.0, shape_full, jnp.float32)
    return 0.25 * (identity + sample * (0.6 / math.sqrt(LOCAL)))


def draw_coarse_inverse(key, part):
    key_off = jax.random.fold_in(key, 31)
    rows_all = jnp.arange(NC, dtype=jnp.int32)
    mode_of = rows_all % MODES
    srow_of = rows_all // MODES % SROWS
    scol_of = rows_all // (MODES * SROWS)
    paired = (srow_of * SCOLS + scol_of) * MODES + mode_of
    identity = (paired[:, None] == rows_all[None, :]).astype(jnp.float32)
    sample = jax.random.truncated_normal(key_off, -6.0, 6.0, (NC, NC), jnp.float32)
    return 4.0 * identity + sample * (2.0 / math.sqrt(NC))


def set_ends(array, key, low, high):
    index_at = [jax.random.randint(jax.random.fold_in(key, axis), (), 0, length) for axis, length in enumerate(array.shape)]
    widest = array.shape.index(max(array.shape))
    neighbour = index_at[:widest] + [(index_at[widest] + 1) % array.shape[widest]] + index_at[widest + 1:]
    return array.at[tuple(index_at)].set(low).at[tuple(neighbour)].set(high)


def block_scale(stream_key, shape, cuts, least, high):
    factor_of = 1.0
    for position, parts in cuts:
        heights = jax.random.uniform(jax.random.fold_in(jax.random.fold_in(stream_key, 6), position), (parts,), jnp.float32, least / len(cuts), high / len(cuts))
        factor_of = factor_of * jnp.repeat(jnp.exp(heights), shape[position] // parts).reshape((-1,) + (1,) * (len(shape) - 1 - position))
    return factor_of


def normal_values(stream_key, dims, scale, reach, shards=(), kind=jnp.bfloat16):
    drawn = scale * jax.random.normal(stream_key, dims, jnp.float32)
    if shards:
        drawn = drawn * block_scale(stream_key, dims, shards, -0.22, 0.18)
    return jnp.clip(drawn, -reach, reach).astype(kind)


def setup_inputs(seed: int = 0) -> dict:
    streams_of = jax.random.split(jax.random.key(seed), 9)
    right_side = draw_right_side(jax.random.fold_in(streams_of[8], 71), 0)
    initial_guess = normal_values(streams_of[1], (NX, NY, NRHS), 1.0, 6.0, ((0, 4), (1, 8)), jnp.float32)
    class_map = set_ends(jax.random.randint(streams_of[2], (NX, NY), 0, CLASSES), jax.random.fold_in(streams_of[2], 1), 0, CLASSES - 1).astype(jnp.int32)
    class_conductivity = jnp.clip(jnp.exp(jax.random.uniform(streams_of[3], (CLASSES,), jnp.float32, math.log(0.2), math.log(2.0))), 0.2, 2.0)
    window_index = jax.vmap(lambda own: jax.random.permutation(own, LOCAL))(jax.random.split(streams_of[4], SROWS * SCOLS)).reshape((SROWS, SCOLS, LOCAL)).astype(jnp.int32)
    local_inverse = draw_local_inverse(jax.random.fold_in(streams_of[8], 71), 0)
    coarse_basis = normal_values(streams_of[6], (SROWS, SCOLS, MODES, LOCAL), LOCAL ** -0.5, 0.1875, ((0, 4), (1, 8)), jnp.float32)
    coarse_inverse = draw_coarse_inverse(jax.random.fold_in(streams_of[8], 71), 0)
    return dict(right_side=right_side, initial_guess=initial_guess, class_map=class_map, class_conductivity=class_conductivity, window_index=window_index, local_inverse=local_inverse, coarse_basis=coarse_basis, coarse_inverse=coarse_inverse)


HIGHEST = lax.Precision.HIGHEST
REACTION = 0.01
NEIGHBOURS = ((0, 1), (2, 1), (1, 0), (1, 2))


def apply_operator(padded_field, conduct):
    height = padded_field.shape[0] - 2
    breadth = padded_field.shape[1] - 2
    centre = padded_field[1:height + 1, 1:breadth + 1]
    own_conduct = conduct[1:height + 1, 1:breadth + 1]
    result = REACTION * centre
    for row_shift, col_shift in NEIGHBOURS:
        beside = padded_field[row_shift:row_shift + height, col_shift:col_shift + breadth]
        face_weight = 0.5 * (own_conduct + conduct[row_shift:row_shift + height, col_shift:col_shift + breadth])
        result = result + face_weight[:, :, None] * (centre - beside)
    return result


def reference(right_side, initial_guess, class_map, class_conductivity, window_index, local_inverse, coarse_basis, coarse_inverse):
    conduct = class_conductivity[class_map]
    conduct_pad = jnp.pad(conduct, 1)

    def operate(values):
        return apply_operator(jnp.pad(values, ((1, 1), (1, 1), (0, 0))), conduct_pad)

    row_index = jnp.arange(SROWS, dtype=jnp.int32)[:, None] * CS + jnp.arange(ES, dtype=jnp.int32)[None, :]
    col_index = jnp.arange(SCOLS, dtype=jnp.int32)[:, None] * CS + jnp.arange(ES, dtype=jnp.int32)[None, :]
    inverse_order = jnp.argsort(window_index, axis=-1).astype(jnp.int32)
    solution = initial_guess
    residual = right_side - operate(solution)
    for iteration in range(ITERS):
        padded_res = jnp.pad(residual, ((OV, OV), (OV, OV), (0, 0)))
        windows = padded_res[row_index[:, None, :, None], col_index[None, :, None, :]]
        windows = windows.reshape(SROWS, SCOLS, ES * ES, NRHS)
        gathered = jnp.take_along_axis(windows, window_index[:, :, :, None], axis=2)
        local_part = jnp.einsum("abkl,ablr->abkr", local_inverse, gathered, precision=HIGHEST)
        coarse_rhs = jnp.einsum("abmk,abkr->abmr", coarse_basis, gathered, precision=HIGHEST).reshape(NC, NRHS)
        coarse_sol = jnp.dot(coarse_inverse, coarse_rhs, precision=HIGHEST, preferred_element_type=jnp.float32)
        coarse_sol = coarse_sol.reshape(SCOLS, SROWS, MODES, NRHS).transpose(1, 0, 2, 3)
        extended = local_part + jnp.einsum("abmk,abmr->abkr", coarse_basis, coarse_sol, precision=HIGHEST)
        windowed = jnp.take_along_axis(extended, inverse_order[:, :, :, None], axis=2)
        windowed = windowed.reshape(SROWS, SCOLS, ES, ES, NRHS)
        direction = windowed[:, :, OV:OV + CS, OV:OV + CS].transpose(0, 2, 1, 3, 4).reshape(NX, NY, NRHS)
        image = operate(direction)
        stepsize = jnp.sum(residual * image, axis=(0, 1)) / jnp.sum(image * image, axis=(0, 1))
        solution = solution + stepsize * direction
        residual = residual - stepsize * image
    return solution, residual
```

```python
import functools
import math

import jax
import jax.numpy as jnp
from jax import lax
from jax.experimental import pallas as pl
from jax.experimental.pallas import tpu as pltpu
from jax.sharding import PartitionSpec as P

ITERS = 3
REACTION = 0.01
LANES = 128
SUB = 8
F32 = jnp.float32
BF16 = jnp.bfloat16
MESH = pl.DeviceIdType.MESH
DIRS = ((-1, -1), (-1, 0), (-1, 1), (0, -1), (0, 1), (1, -1), (1, 0), (1, 1))


def split(value):
    high = value.astype(BF16)
    return high, (value - high.astype(F32)).astype(BF16)


def dot(left, right):
    return jnp.dot(left, right, preferred_element_type=F32)


def dot3(left_high, left_low, right_high, right_low):
    return dot(left_high, right_high) + (dot(left_low, right_high) + dot(left_high, right_low))


def kernel(
    cfg,
    rhs_ref,
    guess_ref,
    cond_ref,
    wrow_ref,
    wcol_ref,
    inv_hbm,
    basis_ref,
    bexp_ref,
    coarse_ref,
    sol_out,
    res_out,
    inv_v,
    perm,
    perm_t,
    t_high,
    t_low,
    l_high,
    l_low,
    x0,
    d0,
    weights,
    phi_high,
    phi_low,
    bw,
    x_high,
    x_low,
    res,
    sol,
    img,
    deep,
    wdeep,
    z,
    kmat,
    g0,
    g,
    row0,
    col0,
    cs0,
    cor0,
    row1,
    col1,
    cs1,
    cor1,
    ssem,
    rsem,
    gs,
    gr,
    fs,
    fr,
    lsem,
):
    N, W, ES, OV, CS, COLS, MODES, KR = cfg
    H = OV + 1
    lo, hi = OV, OV + CS - H
    LOCAL = ES * ES
    DW = ES + 2 * SUB
    DH = ES + 2
    HALF = N // 2
    CHIPS = HALF * W
    a = lax.axis_index("narrow")
    b = lax.axis_index("wide")
    core = lax.rem(a, 2)
    me = (a // 2) * W + b

    def other(k):
        idx = lax.rem(me + k, CHIPS)
        return idx, (lax.rem(idx, W), 2 * (idx // W) + core)

    def valid(d):
        da, db = DIRS[d]
        return (a + da >= 0) & (a + da < N) & (b + db >= 0) & (b + db < W)

    barrier = pltpu.get_barrier_semaphore()

    def greet(k, carry):
        pl.semaphore_signal(barrier, inc=1, device_id=other(k)[1], device_id_type=MESH)
        return carry

    lax.fori_loop(1, CHIPS, greet, 0)
    count = CHIPS - 1
    for d, (da, db) in enumerate(DIRS):
        if da != 0:
            ok = valid(d)
            count = count + ok.astype(jnp.int32)

            @pl.when(ok)
            def _():
                pl.semaphore_signal(barrier, inc=1, device_id=(b + db, a + da), device_id_type=MESH)

    load = pltpu.make_async_copy(inv_hbm, inv_v, lsem)
    load.start()

    for d, (da, db) in enumerate(DIRS):

        @pl.when(jnp.logical_not(valid(d)))
        def _():
            for slot in range(ITERS + 1):
                if slot == 0:
                    rr, cc, kk = row0, col0, cor0
                else:
                    rr, cc, kk = row1.at[slot - 1], col1.at[slot - 1], cor1.at[slot - 1]
                if db == 0:
                    ref = rr.at[(da + 1) // 2]
                elif da == 0:
                    ref = cc.at[(db + 1) // 2]
                else:
                    ref = kk.at[(da + 1) + (db + 1) // 2]
                ref[...] = jnp.zeros(ref.shape, F32)

    step = 256

    def hot(i, carry):
        off = pl.multiple_of(i * step, step)
        pos = lax.broadcasted_iota(jnp.int32, (step, LOCAL), 0) + off
        perm[pl.ds(off, step), :] = jnp.where(pos == wrow_ref[...], 1.0, 0.0).astype(BF16)
        lane = lax.broadcasted_iota(jnp.int32, (step, LOCAL), 1)
        perm_t[pl.ds(off, step), :] = jnp.where(
            lane == wcol_ref[pl.ds(off, step), :], 1.0, 0.0
        ).astype(BF16)
        return carry

    lax.fori_loop(0, LOCAL // step, hot, 0)
    b_high, b_low = split(bexp_ref[...])
    packed = dot(perm[...], b_high) + dot(perm[...], b_low)
    x0[:, :, 2 * COLS :] = packed.reshape(ES, ES, LANES)
    last = lax.broadcasted_iota(jnp.int32, (CS, LANES), 1) == LANES - 1

    def fill(i, carry):
        u = OV + i
        x0[u, OV : OV + CS, 0:COLS] = guess_ref[i]
        x0[u, OV : OV + CS, COLS : 2 * COLS] = rhs_ref[i]
        x0[u, OV : OV + CS, 2 * COLS :] = jnp.where(
            last, cond_ref[i], x0[u, OV : OV + CS, 2 * COLS :]
        )
        return carry

    lax.fori_loop(0, CS, fill, 0)

    def strips(slot, src, rr, cc, cs, kk):
        copies = []
        for d, (da, db) in enumerate(DIRS):
            rows = pl.ds(hi if da > 0 else lo, H)
            if db == 0:
                part, dst = src.at[rows], rr.at[(1 - da) // 2]
            elif da == 0:
                part, dst = cs.at[(db + 1) // 2], cc.at[(1 - db) // 2]
            else:
                part = src.at[rows, pl.ds(ES - SUB if db > 0 else 0, SUB)]
                dst = kk.at[(1 - da) + (1 - db) // 2]
            copies.append(
                pltpu.make_async_remote_copy(
                    src_ref=part,
                    dst_ref=dst,
                    send_sem=ssem.at[slot, d],
                    recv_sem=rsem.at[slot, 7 - d],
                    device_id=(b + db, a + da),
                    device_id_type=MESH,
                )
            )
        return copies

    def pack(src, cs):
        def body(u, carry):
            for j in range(H):
                cs[0, j, pl.ds(u, 1), :] = src[u, lo + j : lo + j + 1, :]
                cs[1, j, pl.ds(u, 1), :] = src[u, hi + j : hi + j + 1, :]
            return carry

        lax.fori_loop(0, ES, body, 0)

    def send_strips(copies):
        for d in (3, 4, 1, 6, 0, 2, 5, 7):

            @pl.when(valid(d))
            def _():
                copies[d].start()

    def recv_strips(copies):
        for d in range(8):

            @pl.when(valid(d))
            def _():
                copies[7 - d].wait_recv()

    def done_strips(copies):
        for d in range(8):

            @pl.when(valid(d))
            def _():
                copies[d].wait_send()

    def unpack(dst, src, rr, cc, kk):
        def centre(i, carry):
            u = OV + i
            dst[u + 1, SUB : SUB + ES, :] = src[u]
            for j in range(H):
                p = SUB - 1 + j
                dst[u + 1, p : p + 1, :] = cc[0, j, pl.ds(u, 1), :]
                p = SUB + CS + OV + j
                dst[u + 1, p : p + 1, :] = cc[1, j, pl.ds(u, 1), :]
            return carry

        lax.fori_loop(0, CS, centre, 0)
        own = slice(OV, OV + CS)
        left, right = SUB - 1, SUB + CS + OV
        base = hi - (ES - SUB)
        for side, top in ((0, 0), (1, CS + H)):
            for j in range(H):
                dst[top + j, SUB + OV : SUB + OV + CS, :] = rr[side, j, own, :]
                dst[top + j, left : left + H, :] = kk[2 * side, j, base : base + H, :]
                dst[top + j, right : right + H, :] = kk[2 * side + 1, j, lo : lo + H, :]

    def coarse_copy(slot, k, ref):
        _, target = other(k)
        return pltpu.make_async_remote_copy(
            src_ref=ref.at[a, b],
            dst_ref=ref.at[a, b],
            send_sem=gs.at[slot, k],
            recv_sem=gr.at[slot, me],
            device_id=target,
            device_id_type=MESH,
        )

    def coarse_send(slot, ref):
        def body(k, carry):
            coarse_copy(slot, k, ref).start()
            return carry

        lax.fori_loop(1, CHIPS, body, 0)

    def forward(slot, i, ref):
        return pltpu.make_async_remote_copy(
            src_ref=ref.at[2 * i + core],
            dst_ref=ref.at[2 * i + core],
            send_sem=fs.at[slot, i],
            recv_sem=fr.at[slot, i],
            device_id=(b, a + 1 - 2 * core),
            device_id_type=MESH,
        )

    def coarse_relay(slot, ref):
        def body(k, carry):
            idx, target = other(k)
            pltpu.make_async_remote_copy(
                src_ref=ref.at[a, b],
                dst_ref=ref.at[target[1], target[0]],
                send_sem=gs.at[slot, k],
                recv_sem=gr.at[slot, idx],
                device_id=target,
                device_id_type=MESH,
            ).wait_recv()
            return carry

        lax.fori_loop(1, CHIPS, body, 0)
        for i in range(HALF):
            forward(slot, i, ref).start()

    def coarse_recv(slot, ref):
        for i in range(HALF):
            pltpu.make_async_remote_copy(
                src_ref=ref.at[2 * i + core],
                dst_ref=ref.at[2 * i + 1 - core],
                send_sem=fs.at[slot, i],
                recv_sem=fr.at[slot, i],
                device_id=(b, a + 1 - 2 * core),
                device_id_type=MESH,
            ).wait_recv()

    def coarse_done(slot, ref):
        def body(k, carry):
            coarse_copy(slot, k, ref).wait_send()
            return carry

        lax.fori_loop(1, CHIPS, body, 0)
        for i in range(HALF):
            forward(slot, i, ref).wait_send()

    first = strips(0, x0, row0, col0, cs0, cor0)
    pack(x0, cs0)
    pl.semaphore_wait(barrier, count)
    send_strips(first)

    load.wait()

    def right_side_perm(i, carry):
        rows = pl.ds(pl.multiple_of(i * step, step), step)
        high, low = split(inv_v[rows, :])
        t_high[rows, :] = dot(high, perm_t[...]).astype(BF16)
        t_low[rows, :] = dot(low, perm_t[...]).astype(BF16)
        return carry

    lax.fori_loop(0, LOCAL // step, right_side_perm, 0)

    def left_side_perm(i, carry):
        rows = pl.ds(pl.multiple_of(i * step, step), step)
        l_high[rows, :] = dot(perm[rows, :], t_high[...]).astype(BF16)
        l_low[rows, :] = dot(perm[rows, :], t_low[...]).astype(BF16)
        return carry

    lax.fori_loop(0, LOCAL // step, left_side_perm, 0)
    m_high, m_low = split(basis_ref[...])
    bw[0] = dot(m_high, perm_t[...]).astype(BF16)
    bw[1] = dot(m_low, perm_t[...]).astype(BF16)

    d0[...] = jnp.zeros(d0.shape, F32)
    recv_strips(first)
    unpack(d0, x0, row0, col0, cor0)

    def modes(u, carry):
        value = d0[u, :, 2 * COLS :]
        high, low = split(value)
        rows = pl.ds(pl.multiple_of(u * DW, DW), DW)
        phi_high[rows, :] = high
        phi_low[rows, :] = low
        d0[u, :, 2 * COLS :] = jnp.broadcast_to(value[:, LANES - 1 : LANES], (DW, LANES))
        return carry

    lax.fori_loop(0, DH, modes, 0)
    col_pos = b * CS - OV + lax.broadcasted_iota(jnp.int32, (ES, LANES), 0)
    col_in = jnp.where((col_pos >= 0) & (col_pos < CS * W), 1.0, 0.0)

    def faces(u, carry):
        row_pos = a * CS - OV + u
        inside = jnp.where((row_pos >= 0) & (row_pos < CS * N), col_in, 0.0)
        cond = lambda du, dt: d0[u + 1 + du, SUB + dt : SUB + dt + ES, 2 * COLS :]
        own = cond(0, 0)
        half = 0.5 * inside
        weights[0, u] = REACTION * inside
        weights[1, u] = half * (own + cond(-1, 0))
        weights[2, u] = half * (own + cond(1, 0))
        weights[3, u] = half * (own + cond(0, -1))
        weights[4, u] = half * (own + cond(0, 1))
        return carry

    lax.fori_loop(0, ES, faces, 0)

    def operator(ref, u):
        parts = []
        for c in range(0, COLS, LANES):
            at = lambda du, dt: ref[u + 1 + du, SUB + dt : SUB + dt + ES, c : c + LANES]
            mid = at(0, 0)
            parts.append(
                weights[0, u] * mid
                + weights[1, u] * (mid - at(-1, 0))
                + weights[2, u] * (mid - at(1, 0))
                + weights[3, u] * (mid - at(0, -1))
                + weights[4, u] * (mid - at(0, 1))
            )
        return jnp.concatenate(parts, axis=1)

    def set_x(u, value):
        high, low = split(value)
        rows = pl.ds(pl.multiple_of(u * ES, ES), ES)
        x_high[rows, :] = high
        x_low[rows, :] = low

    def first_residual(u, carry):
        inside = jnp.where(weights[0, u] > 0.0, 1.0, 0.0)
        inside = jnp.concatenate([inside] * (COLS // LANES), axis=1)
        right = d0[u + 1, SUB : SUB + ES, COLS : 2 * COLS]
        value = right * inside - operator(d0, u)
        res[u] = value
        set_x(u, value)
        return carry

    lax.fori_loop(0, ES, first_residual, 0)

    def start_sol(i, carry):
        sol[i] = d0[OV + i + 1, SUB : SUB + ES, 0:COLS]
        return carry

    lax.fori_loop(0, CS, start_sol, 0)

    def coarse_rows():
        return dot3(bw[0], bw[1], x_high[...], x_low[...])

    sub_pos = lax.broadcasted_iota(jnp.int32, (SUB, COLS), 0)
    wdeep[...] = jnp.zeros(wdeep.shape, F32)
    pending = []
    numer = denom = None
    for it in range(ITERS + 1):
        ref = g0 if it == 0 else g.at[it - 1]
        if it == 0:
            ref[a, b] = jnp.zeros((ref.shape[2], COLS), F32)
            ref[a, b, 0:SUB, :] = coarse_rows()
            ref[a, b, MODES : MODES + KR, :] = coarse_ref[...]
        else:
            rows = coarse_rows() if it < ITERS else jnp.zeros((SUB, COLS), F32)
            rows = jnp.where(sub_pos == MODES, numer, rows)
            rows = jnp.where(sub_pos == MODES + 1, denom, rows)
            ref[a, b] = rows
        coarse_send(it, ref)
        if it < ITERS:

            def solve(i, carry):
                rows = pl.ds(pl.multiple_of(i * step, step), step)
                value = dot3(l_high[rows, :], l_low[rows, :], x_high[...], x_low[...])
                z[it, pl.ds(i * (step // ES), step // ES)] = value.reshape(step // ES, ES, COLS)
                return carry

            lax.fori_loop(0, LOCAL // step, solve, 0)
            pack(z.at[it], cs1.at[it])
            copies = strips(it + 1, z.at[it], row1.at[it], col1.at[it], cs1.at[it], cor1.at[it])
            send_strips(copies)
            pending.append(copies)
        coarse_relay(it, ref)
        coarse_recv(it, ref)
        if it == 0:
            per = COLS // (4 * W)
            wide_cols = MODES * W
            group = MODES * N
            piece = lax.broadcasted_iota(jnp.int32, (group, COLS), 0) & (per - 1)
            lane = lax.broadcasted_iota(jnp.int32, (group, COLS), 1)
            keep = (lane >> int(math.log2(wide_cols))) == piece
            width = N * W * SUB
            j = lax.broadcasted_iota(jnp.int32, (COLS, width), 0) & (wide_cols - 1)
            c = lax.broadcasted_iota(jnp.int32, (COLS, width), 1)
            total_high = total_low = None
            for a2 in range(N):
                blocks = []
                for third in range(3):
                    db = lax.rem(third - b + 1 + 3 * W, 3) - 1
                    at = jnp.clip(b + db, 0, W - 1)
                    raw = ref[a2, at, MODES : MODES + KR, :]
                    tall = jnp.concatenate(
                        [jnp.broadcast_to(raw[r : r + 1], (per, COLS)) for r in range(KR)], axis=0
                    )
                    blocks.append(jnp.where(keep, tall, 0.0))
                blocks.append(jnp.zeros((LANES - 3 * group, COLS), F32))
                high, low = split(jnp.concatenate(blocks, axis=0))
                fold = c == a2 * (W * SUB) + (j >> 2) * SUB + (j & 3)
                fold = jnp.where(fold, 1.0, 0.0).astype(BF16)
                th, tl = dot(high, fold), dot(low, fold)
                total_high = th if total_high is None else total_high + th
                total_low = tl if total_low is None else total_low + tl
            kmat[0] = total_high.astype(BF16)
            kmat[1] = total_low.astype(BF16)
        else:
            total = jnp.sum(ref[...].reshape(N * W, SUB, COLS), axis=0)
            size = total[MODES : MODES + 1] / total[MODES + 1 : MODES + 2]
        if it == ITERS:
            break
        g_high, g_low = split(ref[:, :, 0:SUB, :].reshape(N * W * SUB, COLS))
        s_high, s_low = split(dot3(kmat[0], kmat[1], g_high, g_low))
        recv_strips(copies)
        unpack(wdeep, z.at[it], row1.at[it], col1.at[it], cor1.at[it])

        if it > 0:

            def advance(i, carry):
                u = OV + i
                sol[i] = sol[i] + size * deep[u + 1, SUB : SUB + ES, :]
                res[u] = res[u] - size * img[u]
                return carry

            lax.fori_loop(0, CS, advance, 0)
        chunk = DH // 2

        def coarse_part(i, carry):
            rows = pl.ds(pl.multiple_of(i * chunk * DW, chunk * DW), chunk * DW)
            value = dot3(phi_high[rows, :], phi_low[rows, :], s_high, s_low)
            tall = pl.ds(i * chunk, chunk)
            value = value.reshape(chunk, DW, COLS) + wdeep[tall]
            if it == 0:
                deep[tall] = value
            else:
                deep[tall] = deep[tall] - size * value
            return carry

        lax.fori_loop(0, 2, coarse_part, 0)

        def apply(u, carry):
            top, bottom = carry
            value = operator(deep, u)
            img[u] = value
            if it < ITERS - 1:
                set_x(u, value)
            own = jnp.where((u >= OV) & (u < OV + CS), value, 0.0)
            return top + res[u] * own, bottom + value * own

        nothing = jnp.zeros((ES, COLS), F32)
        top, bottom = lax.fori_loop(0, ES, apply, (nothing, nothing))
        col = lax.broadcasted_iota(jnp.int32, (ES, COLS), 0)
        mine = (col >= OV) & (col < OV + CS)
        numer = jnp.sum(jnp.where(mine, top, 0.0), axis=0, keepdims=True)
        denom = jnp.sum(jnp.where(mine, bottom, 0.0), axis=0, keepdims=True)

    def finish(i, carry):
        u = OV + i
        sol_out[i] = (sol[i] + size * deep[u + 1, SUB : SUB + ES, :])[OV : OV + CS]
        res_out[i] = (res[u] - size * img[u])[OV : OV + CS]
        return carry

    lax.fori_loop(0, CS, finish, 0)
    done_strips(first)
    for copies in pending:
        done_strips(copies)
    for it in range(ITERS + 1):
        coarse_done(it, g0 if it == 0 else g.at[it - 1])


def local(
    N,
    W,
    right_side,
    initial_guess,
    class_map,
    class_conductivity,
    window_index,
    local_inverse,
    coarse_basis,
    coarse_inverse,
):
    CS, _, COLS = right_side.shape
    MODES, LOCAL = coarse_basis.shape[2:]
    ES = math.isqrt(LOCAL)
    OV = (ES - CS) // 2
    H = OV + 1
    DW, DH = ES + 2 * SUB, ES + 2
    KR = coarse_inverse.size // COLS
    R0 = -(-(MODES + KR) // SUB) * SUB
    CHIPS = N * W // 2
    classes = class_conductivity.shape[0]
    matches = class_map[:, :, None] == jnp.arange(classes, dtype=jnp.int32)[None, None, :]
    conduct = jnp.sum(jnp.where(matches, class_conductivity[None, None, :], 0.0), axis=2)
    conduct = jnp.broadcast_to(conduct[:, :, None], (CS, CS, LANES))
    basis = coarse_basis[0, 0]
    place = lax.rem(lax.axis_index("wide"), 3) * (MODES * N) + lax.axis_index("narrow") * MODES
    lane = jnp.arange(LANES, dtype=jnp.int32)[None, :] - place
    turned = basis.T
    spread = sum(jnp.where(lane == m, turned[:, m : m + 1], 0.0) for m in range(MODES))
    padded = jnp.concatenate([basis, jnp.zeros((SUB - MODES, LOCAL), F32)], axis=0)
    vmem = pl.BlockSpec(memory_space=pltpu.VMEM)
    big = 2 * COLS + LANES
    scratch = [
        pltpu.VMEM((LOCAL, LOCAL), F32),
        pltpu.VMEM((LOCAL, LOCAL), BF16),
        pltpu.VMEM((LOCAL, LOCAL), BF16),
        pltpu.VMEM((LOCAL, LOCAL), BF16),
        pltpu.VMEM((LOCAL, LOCAL), BF16),
        pltpu.VMEM((LOCAL, LOCAL), BF16),
        pltpu.VMEM((LOCAL, LOCAL), BF16),
        pltpu.VMEM((ES, ES, big), F32),
        pltpu.VMEM((DH, DW, big), F32),
        pltpu.VMEM((5, ES, ES, LANES), F32),
        pltpu.VMEM((DH * DW, LANES), BF16),
        pltpu.VMEM((DH * DW, LANES), BF16),
        pltpu.VMEM((2, SUB, LOCAL), BF16),
        pltpu.VMEM((LOCAL, COLS), BF16),
        pltpu.VMEM((LOCAL, COLS), BF16),
        pltpu.VMEM((ES, ES, COLS), F32),
        pltpu.VMEM((CS, ES, COLS), F32),
        pltpu.VMEM((ES, ES, COLS), F32),
        pltpu.VMEM((DH, DW, COLS), F32),
        pltpu.VMEM((DH, DW, COLS), F32),
        pltpu.VMEM((ITERS, ES, ES, COLS), F32),
        pltpu.VMEM((2, LANES, N * W * SUB), BF16),
        pltpu.VMEM((N, W, R0, COLS), F32),
        pltpu.VMEM((ITERS, N, W, SUB, COLS), F32),
        pltpu.VMEM((2, H, ES, big), F32),
        pltpu.VMEM((2, H, ES, big), F32),
        pltpu.VMEM((2, H, ES, big), F32),
        pltpu.VMEM((4, H, SUB, big), F32),
        pltpu.VMEM((ITERS, 2, H, ES, COLS), F32),
        pltpu.VMEM((ITERS, 2, H, ES, COLS), F32),
        pltpu.VMEM((ITERS, 2, H, ES, COLS), F32),
        pltpu.VMEM((ITERS, 4, H, SUB, COLS), F32),
        pltpu.SemaphoreType.DMA((ITERS + 1, 8)),
        pltpu.SemaphoreType.DMA((ITERS + 1, 8)),
        pltpu.SemaphoreType.DMA((ITERS + 1, CHIPS)),
        pltpu.SemaphoreType.DMA((ITERS + 1, CHIPS)),
        pltpu.SemaphoreType.DMA((ITERS + 1, N // 2)),
        pltpu.SemaphoreType.DMA((ITERS + 1, N // 2)),
        pltpu.SemaphoreType.DMA,
    ]
    out = jax.ShapeDtypeStruct(right_side.shape, F32)
    return pl.pallas_call(
        functools.partial(kernel, (N, W, ES, OV, CS, COLS, MODES, KR)),
        out_shape=(out, out),
        in_specs=[vmem] * 5 + [pl.BlockSpec(memory_space=pl.ANY)] + [vmem] * 3,
        out_specs=(vmem, vmem),
        scratch_shapes=scratch,
        compiler_params=pltpu.CompilerParams(
            collective_id=0, has_side_effects=True, vmem_limit_bytes=67043328
        ),
        name="schwarz",
    )(
        right_side,
        initial_guess,
        conduct,
        window_index.reshape(1, LOCAL),
        window_index.reshape(LOCAL, 1),
        local_inverse[0, 0],
        padded,
        spread,
        coarse_inverse.reshape(KR, COLS),
    )


def solution(mesh):
    in_specs = (
        P("narrow", "wide", None),
        P("narrow", "wide", None),
        P("narrow", "wide"),
        P(),
        P("narrow", "wide", None),
        P("narrow", "wide", None, None),
        P("narrow", "wide", None, None),
        P("wide", "narrow"),
    )
    out_specs = (P("narrow", "wide", None), P("narrow", "wide", None))
    body = functools.partial(local, mesh.shape["narrow"], mesh.shape["wide"])
    return jax.shard_map(body, mesh=mesh, in_specs=in_specs, out_specs=out_specs, check_vma=False)
```

```python
import functools
import math

import jax
import jax.numpy as jnp
from jax import lax
from jax.experimental import pallas as pl
from jax.experimental.pallas import tpu as pltpu
from jax.sharding import PartitionSpec as P

ITERS = 3
REACTION = 0.01
LANES = 128
SUB = 8
F32 = jnp.float32
BF16 = jnp.bfloat16
MESH = pl.DeviceIdType.MESH
DIRS = ((-1, -1), (-1, 0), (-1, 1), (0, -1), (0, 1), (1, -1), (1, 0), (1, 1))


def split(value):
    high = value.astype(BF16)
    return high, (value - high.astype(F32)).astype(BF16)


def dot(left, right):
    return jnp.dot(left, right, preferred_element_type=F32)


def dot3(left_high, left_low, right_high, right_low):
    return dot(left_high, right_high) + (dot(left_low, right_high) + dot(left_high, right_low))


def kernel(
    cfg,
    rhs_ref,
    guess_ref,
    map_ref,
    class_ref,
    wrow_ref,
    inv_hbm,
    basis_ref,
    coarse_ref,
    sol_out,
    dir_out,
    res_out,
    img_out,
    size_out,
    inv_v,
    perm,
    perm_t,
    t_high,
    t_low,
    l_high,
    l_low,
    x0,
    d0,
    weights,
    phi_high,
    phi_low,
    bw,
    x_high,
    x_low,
    res,
    sol,
    img,
    deep,
    wdeep,
    z,
    kmat,
    g0,
    g,
    row0,
    col0,
    cs0,
    cor0,
    row1,
    col1,
    cs1,
    cor1,
    ssem,
    rsem,
    gs,
    gr,
    fs,
    fr,
    lsem,
    osem,
    field,
    spread,
):
    N, W, ES, OV, CS, COLS, MODES, KR = cfg
    H = OV + 1
    lo, hi = OV, OV + CS - H
    LOCAL = ES * ES
    DW = ES + 2 * SUB
    DH = ES + 2
    HALF = N // 2
    CHIPS = HALF * W
    a = lax.axis_index("narrow")
    b = lax.axis_index("wide")
    core = lax.rem(a, 2)
    me = (a // 2) * W + b

    def other(k):
        idx = lax.rem(me + k, CHIPS)
        return idx, (lax.rem(idx, W), 2 * (idx // W) + core)

    def valid(d):
        da, db = DIRS[d]
        return (a + da >= 0) & (a + da < N) & (b + db >= 0) & (b + db < W)

    barrier = pltpu.get_barrier_semaphore()

    def greet(k, carry):
        pl.semaphore_signal(barrier, inc=1, device_id=other(k)[1], device_id_type=MESH)
        return carry

    lax.fori_loop(1, CHIPS, greet, 0)
    count = CHIPS - 1
    for d, (da, db) in enumerate(DIRS):
        if da != 0:
            ok = valid(d)
            count = count + ok.astype(jnp.int32)

            @pl.when(ok)
            def _():
                pl.semaphore_signal(barrier, inc=1, device_id=(b + db, a + da), device_id_type=MESH)

    load = pltpu.make_async_copy(inv_hbm, inv_v, lsem)
    load.start()

    for d, (da, db) in enumerate(DIRS):

        @pl.when(jnp.logical_not(valid(d)))
        def _():
            for slot in range(ITERS + 1):
                if slot == 0:
                    rr, cc, kk = row0, col0, cor0
                else:
                    rr, cc, kk = row1.at[slot - 1], col1.at[slot - 1], cor1.at[slot - 1]
                if db == 0:
                    ref = rr.at[(da + 1) // 2]
                elif da == 0:
                    ref = cc.at[(db + 1) // 2]
                else:
                    ref = kk.at[(da + 1) + (db + 1) // 2]
                ref[...] = jnp.zeros(ref.shape, F32)

    step = 256
    numbering = wrow_ref[...]
    tall_numbering = jnp.transpose(jnp.broadcast_to(numbering, (LANES, LOCAL)))
    lane = lax.broadcasted_iota(jnp.int32, (LOCAL, LANES), 1)
    for c in range(0, LOCAL, LANES):
        perm_t[:, c : c + LANES] = jnp.where(lane + c == tall_numbering, 1.0, 0.0).astype(BF16)

    def hot(i, carry):
        off = pl.multiple_of(i * step, step)
        pos = lax.broadcasted_iota(jnp.int32, (step, LOCAL), 0) + off
        perm[pl.ds(off, step), :] = jnp.where(pos == numbering, 1.0, 0.0).astype(BF16)
        return carry

    lax.fori_loop(0, LOCAL // step, hot, 0)
    basis = basis_ref[0, 0]
    place = lax.rem(b, 3) * (MODES * N) + a * MODES
    line = lax.broadcasted_iota(jnp.int32, (LANES, LOCAL), 0) - place
    spread[...] = jnp.zeros(spread.shape, F32)
    for m in range(MODES):
        spread[...] = jnp.where(line == m, basis[m : m + 1], spread[...])
    b_high, b_low = split(jnp.transpose(spread[...]))
    packed = dot(perm[...], b_high) + dot(perm[...], b_low)
    x0[:, :, 2 * COLS :] = packed.reshape(ES, ES, LANES)
    classes = map_ref[...]
    conduct = jnp.zeros(classes.shape, F32)
    for k in range(class_ref.shape[0]):
        conduct = jnp.where(classes == k, class_ref[k], conduct)
    field[...] = jnp.zeros(field.shape, F32)
    field[0:CS, 0:CS] = conduct
    turned = jnp.transpose(field[...])[0:ES]
    lanes = lax.broadcasted_iota(jnp.int32, (ES, LANES), 1)
    last = lax.broadcasted_iota(jnp.int32, (CS, LANES), 1) == LANES - 1

    def fill(i, carry):
        u = OV + i
        column = jnp.sum(jnp.where(lanes == i, turned, 0.0), axis=1, keepdims=True)
        x0[u, OV : OV + CS, 0:COLS] = guess_ref[i]
        x0[u, OV : OV + CS, COLS : 2 * COLS] = rhs_ref[i]
        x0[u, OV : OV + CS, 2 * COLS :] = jnp.where(
            last, column[0:CS], x0[u, OV : OV + CS, 2 * COLS :]
        )
        return carry

    lax.fori_loop(0, CS, fill, 0)

    def strips(slot, src, rr, cc, cs, kk):
        copies = []
        for d, (da, db) in enumerate(DIRS):
            rows = pl.ds(hi if da > 0 else lo, H)
            if db == 0:
                part, dst = src.at[rows], rr.at[(1 - da) // 2]
            elif da == 0:
                part, dst = cs.at[(db + 1) // 2], cc.at[(1 - db) // 2]
            else:
                part = src.at[rows, pl.ds(ES - SUB if db > 0 else 0, SUB)]
                dst = kk.at[(1 - da) + (1 - db) // 2]
            copies.append(
                pltpu.make_async_remote_copy(
                    src_ref=part,
                    dst_ref=dst,
                    send_sem=ssem.at[slot, d],
                    recv_sem=rsem.at[slot, 7 - d],
                    device_id=(b + db, a + da),
                    device_id_type=MESH,
                )
            )
        return copies

    def pack(src, cs):
        def body(u, carry):
            for j in range(H):
                cs[0, j, pl.ds(u, 1), :] = src[u, lo + j : lo + j + 1, :]
                cs[1, j, pl.ds(u, 1), :] = src[u, hi + j : hi + j + 1, :]
            return carry

        lax.fori_loop(0, ES, body, 0)

    def send_strips(copies):
        for d in (3, 4, 1, 6, 0, 2, 5, 7):

            @pl.when(valid(d))
            def _():
                copies[d].start()

    def recv_strips(copies):
        for d in range(8):

            @pl.when(valid(d))
            def _():
                copies[7 - d].wait_recv()

    def done_strips(copies):
        for d in range(8):

            @pl.when(valid(d))
            def _():
                copies[d].wait_send()

    def unpack(dst, src, rr, cc, kk):
        def centre(i, carry):
            u = OV + i
            dst[u + 1, SUB : SUB + ES, :] = src[u]
            for j in range(H):
                p = SUB - 1 + j
                dst[u + 1, p : p + 1, :] = cc[0, j, pl.ds(u, 1), :]
                p = SUB + CS + OV + j
                dst[u + 1, p : p + 1, :] = cc[1, j, pl.ds(u, 1), :]
            return carry

        lax.fori_loop(0, CS, centre, 0)
        own = slice(OV, OV + CS)
        left, right = SUB - 1, SUB + CS + OV
        base = hi - (ES - SUB)
        for side, top in ((0, 0), (1, CS + H)):
            for j in range(H):
                dst[top + j, SUB + OV : SUB + OV + CS, :] = rr[side, j, own, :]
                dst[top + j, left : left + H, :] = kk[2 * side, j, base : base + H, :]
                dst[top + j, right : right + H, :] = kk[2 * side + 1, j, lo : lo + H, :]

    def coarse_copy(slot, k, ref):
        _, target = other(k)
        return pltpu.make_async_remote_copy(
            src_ref=ref.at[a, b],
            dst_ref=ref.at[a, b],
            send_sem=gs.at[slot, k],
            recv_sem=gr.at[slot, me],
            device_id=target,
            device_id_type=MESH,
        )

    def coarse_send(slot, ref):
        def body(k, carry):
            coarse_copy(slot, k, ref).start()
            return carry

        lax.fori_loop(1, CHIPS, body, 0)

    def forward(slot, i, ref):
        return pltpu.make_async_remote_copy(
            src_ref=ref.at[2 * i + core],
            dst_ref=ref.at[2 * i + core],
            send_sem=fs.at[slot, i],
            recv_sem=fr.at[slot, i],
            device_id=(b, a + 1 - 2 * core),
            device_id_type=MESH,
        )

    def coarse_relay(slot, ref):
        def body(k, carry):
            idx, target = other(k)
            pltpu.make_async_remote_copy(
                src_ref=ref.at[a, b],
                dst_ref=ref.at[target[1], target[0]],
                send_sem=gs.at[slot, k],
                recv_sem=gr.at[slot, idx],
                device_id=target,
                device_id_type=MESH,
            ).wait_recv()
            return carry

        lax.fori_loop(1, CHIPS, body, 0)
        for i in range(HALF):
            forward(slot, i, ref).start()

    def coarse_recv(slot, ref):
        for i in range(HALF):
            pltpu.make_async_remote_copy(
                src_ref=ref.at[2 * i + core],
                dst_ref=ref.at[2 * i + 1 - core],
                send_sem=fs.at[slot, i],
                recv_sem=fr.at[slot, i],
                device_id=(b, a + 1 - 2 * core),
                device_id_type=MESH,
            ).wait_recv()

    def coarse_done(slot, ref):
        def body(k, carry):
            coarse_copy(slot, k, ref).wait_send()
            return carry

        lax.fori_loop(1, CHIPS, body, 0)
        for i in range(HALF):
            forward(slot, i, ref).wait_send()

    first = strips(0, x0, row0, col0, cs0, cor0)
    pack(x0, cs0)
    pl.semaphore_wait(barrier, count)
    send_strips(first)
    d0[...] = jnp.zeros(d0.shape, F32)
    wdeep[...] = jnp.zeros(wdeep.shape, F32)

    load.wait()

    def right_side_perm(i, carry):
        rows = pl.ds(pl.multiple_of(i * step, step), step)
        high, low = split(inv_v[rows, :])
        t_high[rows, :] = dot(high, perm_t[...]).astype(BF16)
        t_low[rows, :] = dot(low, perm_t[...]).astype(BF16)
        return carry

    lax.fori_loop(0, LOCAL // step, right_side_perm, 0)

    def left_side_perm(i, carry):
        rows = pl.ds(pl.multiple_of(i * step, step), step)
        l_high[rows, :] = dot(perm[rows, :], t_high[...]).astype(BF16)
        l_low[rows, :] = dot(perm[rows, :], t_low[...]).astype(BF16)
        return carry

    lax.fori_loop(0, LOCAL // step, left_side_perm, 0)
    m_high, m_low = split(jnp.concatenate([basis, jnp.zeros((SUB - MODES, LOCAL), F32)], axis=0))
    bw[0] = dot(m_high, perm_t[...]).astype(BF16)
    bw[1] = dot(m_low, perm_t[...]).astype(BF16)

    recv_strips(first)
    unpack(d0, x0, row0, col0, cor0)

    def modes(u, carry):
        value = d0[u, :, 2 * COLS :]
        high, low = split(value)
        rows = pl.ds(pl.multiple_of(u * DW, DW), DW)
        phi_high[rows, :] = high
        phi_low[rows, :] = low
        d0[u, :, 2 * COLS :] = jnp.broadcast_to(value[:, LANES - 1 : LANES], (DW, LANES))
        return carry

    lax.fori_loop(0, DH, modes, 0)
    col_pos = b * CS - OV + lax.broadcasted_iota(jnp.int32, (ES, LANES), 0)
    col_in = jnp.where((col_pos >= 0) & (col_pos < CS * W), 1.0, 0.0)

    def faces(u, carry):
        row_pos = a * CS - OV + u
        inside = jnp.where((row_pos >= 0) & (row_pos < CS * N), col_in, 0.0)
        cond = lambda du, dt: d0[u + 1 + du, SUB + dt : SUB + dt + ES, 2 * COLS :]
        own = cond(0, 0)
        half = 0.5 * inside
        weights[0, u] = REACTION * inside
        weights[1, u] = half * (own + cond(-1, 0))
        weights[2, u] = half * (own + cond(1, 0))
        weights[3, u] = half * (own + cond(0, -1))
        weights[4, u] = half * (own + cond(0, 1))
        return carry

    lax.fori_loop(0, ES, faces, 0)

    def operator(ref, u):
        parts = []
        for c in range(0, COLS, LANES):
            at = lambda du, dt: ref[u + 1 + du, SUB + dt : SUB + dt + ES, c : c + LANES]
            mid = at(0, 0)
            parts.append(
                weights[0, u] * mid
                + weights[1, u] * (mid - at(-1, 0))
                + weights[2, u] * (mid - at(1, 0))
                + weights[3, u] * (mid - at(0, -1))
                + weights[4, u] * (mid - at(0, 1))
            )
        return jnp.concatenate(parts, axis=1)

    def set_x(u, value):
        high, low = split(value)
        rows = pl.ds(pl.multiple_of(u * ES, ES), ES)
        x_high[rows, :] = high
        x_low[rows, :] = low

    def first_residual(u, carry):
        inside = jnp.where(weights[0, u] > 0.0, 1.0, 0.0)
        inside = jnp.concatenate([inside] * (COLS // LANES), axis=1)
        right = d0[u + 1, SUB : SUB + ES, COLS : 2 * COLS]
        value = right * inside - operator(d0, u)
        res[u] = value
        set_x(u, value)
        return carry

    lax.fori_loop(0, ES, first_residual, 0)

    def start_sol(i, carry):
        sol[i] = d0[OV + i + 1, SUB : SUB + ES, 0:COLS]
        return carry

    lax.fori_loop(0, CS, start_sol, 0)

    def coarse_rows():
        return dot3(bw[0], bw[1], x_high[...], x_low[...])

    sub_pos = lax.broadcasted_iota(jnp.int32, (SUB, COLS), 0)
    pending = []
    numer = denom = None
    for it in range(ITERS + 1):
        ref = g0 if it == 0 else g.at[it - 1]
        if it == 0:
            ref[a, b] = jnp.zeros((ref.shape[2], COLS), F32)
            ref[a, b, 0:SUB, :] = coarse_rows()
            run = MODES * W
            for i in range(MODES * N):
                line, at = divmod(i * run, COLS)
                ref[a, b, MODES + line, at : at + run] = coarse_ref[i]
        else:
            rows = coarse_rows() if it < ITERS else jnp.zeros((SUB, COLS), F32)
            rows = jnp.where(sub_pos == MODES, numer, rows)
            rows = jnp.where(sub_pos == MODES + 1, denom, rows)
            ref[a, b] = rows
        coarse_send(it, ref)
        if it == ITERS:
            own = pl.ds(OV, CS)
            pairs = (
                (sol, sol_out),
                (deep.at[pl.ds(OV + 1, CS), pl.ds(SUB, ES)], dir_out),
                (res.at[own], res_out),
                (img.at[own], img_out),
            )
            writes = [
                pltpu.make_async_copy(src, dst, osem.at[n]) for n, (src, dst) in enumerate(pairs)
            ]
            for copy in writes:
                copy.start()
        if it < ITERS:

            def solve(i, carry):
                rows = pl.ds(pl.multiple_of(i * step, step), step)
                value = dot3(l_high[rows, :], l_low[rows, :], x_high[...], x_low[...])
                z[it, pl.ds(i * (step // ES), step // ES)] = value.reshape(step // ES, ES, COLS)
                return carry

            lax.fori_loop(0, LOCAL // step, solve, 0)
            pack(z.at[it], cs1.at[it])
            copies = strips(it + 1, z.at[it], row1.at[it], col1.at[it], cs1.at[it], cor1.at[it])
            send_strips(copies)
            pending.append(copies)
        coarse_relay(it, ref)
        coarse_recv(it, ref)
        if it == 0:
            per = COLS // (4 * W)
            wide_cols = MODES * W
            group = MODES * N
            piece = lax.broadcasted_iota(jnp.int32, (group, COLS), 0) & (per - 1)
            lane = lax.broadcasted_iota(jnp.int32, (group, COLS), 1)
            keep = (lane >> int(math.log2(wide_cols))) == piece
            width = N * W * SUB
            j = lax.broadcasted_iota(jnp.int32, (COLS, width), 0) & (wide_cols - 1)
            c = lax.broadcasted_iota(jnp.int32, (COLS, width), 1)
            total_high = total_low = None
            for a2 in range(N):
                blocks = []
                for third in range(3):
                    db = lax.rem(third - b + 1 + 3 * W, 3) - 1
                    at = jnp.clip(b + db, 0, W - 1)
                    raw = ref[a2, at, MODES : MODES + KR, :]
                    tall = jnp.concatenate(
                        [jnp.broadcast_to(raw[r : r + 1], (per, COLS)) for r in range(KR)], axis=0
                    )
                    blocks.append(jnp.where(keep, tall, 0.0))
                blocks.append(jnp.zeros((LANES - 3 * group, COLS), F32))
                high, low = split(jnp.concatenate(blocks, axis=0))
                fold = c == a2 * (W * SUB) + (j >> 2) * SUB + (j & 3)
                fold = jnp.where(fold, 1.0, 0.0).astype(BF16)
                th, tl = dot(high, fold), dot(low, fold)
                total_high = th if total_high is None else total_high + th
                total_low = tl if total_low is None else total_low + tl
            kmat[0] = total_high.astype(BF16)
            kmat[1] = total_low.astype(BF16)
        else:
            total = jnp.sum(ref[...].reshape(N * W, SUB, COLS), axis=0)
            size = total[MODES : MODES + 1] / total[MODES + 1 : MODES + 2]
        if it == ITERS:
            break
        g_high, g_low = split(ref[:, :, 0:SUB, :].reshape(N * W * SUB, COLS))
        s_high, s_low = split(dot3(kmat[0], kmat[1], g_high, g_low))
        recv_strips(copies)
        unpack(wdeep, z.at[it], row1.at[it], col1.at[it], cor1.at[it])

        if it > 0:

            def advance(i, carry):
                u = OV + i
                sol[i] = sol[i] + size * deep[u + 1, SUB : SUB + ES, :]
                res[u] = res[u] - size * img[u]
                return carry

            lax.fori_loop(0, CS, advance, 0)
        chunk = DH // 2

        def coarse_part(i, carry):
            rows = pl.ds(pl.multiple_of(i * chunk * DW, chunk * DW), chunk * DW)
            value = dot3(phi_high[rows, :], phi_low[rows, :], s_high, s_low)
            tall = pl.ds(i * chunk, chunk)
            value = value.reshape(chunk, DW, COLS) + wdeep[tall]
            if it == 0:
                deep[tall] = value
            else:
                deep[tall] = deep[tall] - size * value
            return carry

        lax.fori_loop(0, 2, coarse_part, 0)

        def apply(u, carry):
            top, bottom = carry
            value = operator(deep, u)
            img[u] = value
            if it < ITERS - 1:
                set_x(u, value)
            own = jnp.where((u >= OV) & (u < OV + CS), value, 0.0)
            return top + res[u] * own, bottom + value * own

        nothing = jnp.zeros((ES, COLS), F32)
        top, bottom = lax.fori_loop(0, ES, apply, (nothing, nothing))
        col = lax.broadcasted_iota(jnp.int32, (ES, COLS), 0)
        mine = (col >= OV) & (col < OV + CS)
        numer = jnp.sum(jnp.where(mine, top, 0.0), axis=0, keepdims=True)
        denom = jnp.sum(jnp.where(mine, bottom, 0.0), axis=0, keepdims=True)

    done_strips(first)
    for copies in pending:
        done_strips(copies)
    size_out[...] = jnp.broadcast_to(size, (SUB, COLS))
    for copy in writes:
        copy.wait()
    for it in range(ITERS + 1):
        coarse_done(it, g0 if it == 0 else g.at[it - 1])


def finish(OV, CS, sol, direction, res, image, size, sol_out, res_out):
    step = size[0:1]
    for i in range(sol.shape[0]):
        sol_out[i] = (sol[i] + step * direction[i])[OV : OV + CS]
        res_out[i] = (res[i] - step * image[i])[OV : OV + CS]


def local(
    N,
    W,
    right_side,
    initial_guess,
    class_map,
    class_conductivity,
    window_index,
    local_inverse,
    coarse_basis,
    coarse_inverse,
):
    CS, _, COLS = right_side.shape
    MODES, LOCAL = coarse_basis.shape[2:]
    ES = math.isqrt(LOCAL)
    OV = (ES - CS) // 2
    H = OV + 1
    DW, DH = ES + 2 * SUB, ES + 2
    KR = coarse_inverse.size // COLS
    R0 = -(-(MODES + KR) // SUB) * SUB
    CHIPS = N * W // 2
    vmem = pl.BlockSpec(memory_space=pltpu.VMEM)
    big = 2 * COLS + LANES
    scratch = [
        pltpu.VMEM((LOCAL, LOCAL), F32),
        pltpu.VMEM((LOCAL, LOCAL), BF16),
        pltpu.VMEM((LOCAL, LOCAL), BF16),
        pltpu.VMEM((LOCAL, LOCAL), BF16),
        pltpu.VMEM((LOCAL, LOCAL), BF16),
        pltpu.VMEM((LOCAL, LOCAL), BF16),
        pltpu.VMEM((LOCAL, LOCAL), BF16),
        pltpu.VMEM((ES, ES, big), F32),
        pltpu.VMEM((DH, DW, big), F32),
        pltpu.VMEM((5, ES, ES, LANES), F32),
        pltpu.VMEM((DH * DW, LANES), BF16),
        pltpu.VMEM((DH * DW, LANES), BF16),
        pltpu.VMEM((2, SUB, LOCAL), BF16),
        pltpu.VMEM((LOCAL, COLS), BF16),
        pltpu.VMEM((LOCAL, COLS), BF16),
        pltpu.VMEM((ES, ES, COLS), F32),
        pltpu.VMEM((CS, ES, COLS), F32),
        pltpu.VMEM((ES, ES, COLS), F32),
        pltpu.VMEM((DH, DW, COLS), F32),
        pltpu.VMEM((DH, DW, COLS), F32),
        pltpu.VMEM((ITERS, ES, ES, COLS), F32),
        pltpu.VMEM((2, LANES, N * W * SUB), BF16),
        pltpu.VMEM((N, W, R0, COLS), F32),
        pltpu.VMEM((ITERS, N, W, SUB, COLS), F32),
        pltpu.VMEM((2, H, ES, big), F32),
        pltpu.VMEM((2, H, ES, big), F32),
        pltpu.VMEM((2, H, ES, big), F32),
        pltpu.VMEM((4, H, SUB, big), F32),
        pltpu.VMEM((ITERS, 2, H, ES, COLS), F32),
        pltpu.VMEM((ITERS, 2, H, ES, COLS), F32),
        pltpu.VMEM((ITERS, 2, H, ES, COLS), F32),
        pltpu.VMEM((ITERS, 4, H, SUB, COLS), F32),
        pltpu.SemaphoreType.DMA((ITERS + 1, 8)),
        pltpu.SemaphoreType.DMA((ITERS + 1, 8)),
        pltpu.SemaphoreType.DMA((ITERS + 1, CHIPS)),
        pltpu.SemaphoreType.DMA((ITERS + 1, CHIPS)),
        pltpu.SemaphoreType.DMA((ITERS + 1, N // 2)),
        pltpu.SemaphoreType.DMA((ITERS + 1, N // 2)),
        pltpu.SemaphoreType.DMA,
        pltpu.SemaphoreType.DMA((4,)),
        pltpu.VMEM((LANES, LANES), F32),
        pltpu.VMEM((LANES, LOCAL), F32),
    ]
    out = jax.ShapeDtypeStruct((CS, ES, COLS), F32)
    anywhere = pl.BlockSpec(memory_space=pl.ANY)
    smem = pl.BlockSpec(memory_space=pltpu.SMEM)
    *fields, size = pl.pallas_call(
        functools.partial(kernel, (N, W, ES, OV, CS, COLS, MODES, KR)),
        out_shape=(out,) * 4 + (jax.ShapeDtypeStruct((SUB, COLS), F32),),
        in_specs=[vmem] * 3 + [smem, vmem, anywhere] + [vmem] * 2,
        out_specs=(anywhere,) * 4 + (vmem,),
        scratch_shapes=scratch,
        compiler_params=pltpu.CompilerParams(
            collective_id=0, has_side_effects=True, vmem_limit_bytes=60 * 2**20
        ),
        name="schwarz",
    )(
        right_side,
        initial_guess,
        class_map,
        class_conductivity,
        window_index[0],
        local_inverse[0, 0],
        coarse_basis,
        coarse_inverse,
    )
    block = CS // 4
    part = pl.BlockSpec((block, ES, COLS), lambda i: (i, 0, 0))
    done = pl.BlockSpec((block, CS, COLS), lambda i: (i, 0, 0))
    return pl.pallas_call(
        functools.partial(finish, OV, CS),
        grid=(CS // block,),
        out_shape=(jax.ShapeDtypeStruct(right_side.shape, F32),) * 2,
        in_specs=[part] * 4 + [pl.BlockSpec((SUB, COLS), lambda i: (0, 0))],
        out_specs=(done, done),
        name="finish",
    )(*fields, size)


def solution(mesh):
    in_specs = (
        P("narrow", "wide", None),
        P("narrow", "wide", None),
        P("narrow", "wide"),
        P(),
        P("narrow", "wide", None),
        P("narrow", "wide", None, None),
        P("narrow", "wide", None, None),
        P("wide", "narrow"),
    )
    out_specs = (P("narrow", "wide", None), P("narrow", "wide", None))
    body = functools.partial(local, mesh.shape["narrow"], mesh.shape["wide"])
    return jax.shard_map(body, mesh=mesh, in_specs=in_specs, out_specs=out_specs, check_vma=False)
```

```python
import functools
import math

import jax
import jax.numpy as jnp
from jax import lax
from jax.experimental import pallas as pl
from jax.experimental.pallas import tpu as pltpu
from jax.sharding import PartitionSpec as P

ITERS = 3
REACTION = 0.01
LANES = 128
SUB = 8
F32 = jnp.float32
BF16 = jnp.bfloat16
MESH = pl.DeviceIdType.MESH
DIRS = ((-1, -1), (-1, 0), (-1, 1), (0, -1), (0, 1), (1, -1), (1, 0), (1, 1))

SIDES = (3, 4, 0, 2, 5, 7)
ENDS = (1, 6)


def split(value):
    high = value.astype(BF16)
    return high, (value - high.astype(F32)).astype(BF16)


def dot(left, right):
    return jnp.dot(left, right, preferred_element_type=F32)


def dot3(left_high, left_low, right_high, right_low):
    return dot(left_high, right_high) + (dot(left_low, right_high) + dot(left_high, right_low))


def kernel(
    cfg,
    rhs_ref,
    guess_ref,
    map_ref,
    class_ref,
    wrow_ref,
    inv_hbm,
    basis_ref,
    coarse_ref,
    sol_out,
    dir_out,
    res_out,
    img_out,
    size_out,
    inv_v,
    perm,
    perm_t,
    t_high,
    t_low,
    l_high,
    l_low,
    x0,
    d0,
    weights,
    phi_high,
    phi_low,
    bw,
    x_high,
    x_low,
    res,
    sol,
    img,
    deep,
    wdeep,
    z,
    kmat,
    g0,
    g,
    row0,
    col0,
    cs0,
    cor0,
    row1,
    col1,
    cs1,
    cor1,
    ssem,
    rsem,
    gs,
    gr,
    fs,
    fr,
    lsem,
    osem,
    field,
    spread,
    e_high,
    e_low,
):
    N, W, ES, OV, CS, COLS, MODES, KR = cfg
    H = OV + 1
    lo, hi = OV, OV + CS - H
    LOCAL = ES * ES
    DW = ES + 2 * SUB
    DH = ES + 2
    HALF = N // 2
    CHIPS = HALF * W
    a = lax.axis_index("narrow")
    b = lax.axis_index("wide")
    core = lax.rem(a, 2)
    me = (a // 2) * W + b

    def other(k):
        idx = lax.rem(me + k, CHIPS)
        return idx, (lax.rem(idx, W), 2 * (idx // W) + core)

    def valid(d):
        da, db = DIRS[d]
        return (a + da >= 0) & (a + da < N) & (b + db >= 0) & (b + db < W)

    barrier = pltpu.get_barrier_semaphore()

    def greet(k, carry):
        pl.semaphore_signal(barrier, inc=1, device_id=other(k)[1], device_id_type=MESH)
        return carry

    lax.fori_loop(1, CHIPS, greet, 0)
    count = CHIPS - 1
    for d, (da, db) in enumerate(DIRS):
        if da != 0:
            ok = valid(d)
            count = count + ok.astype(jnp.int32)

            @pl.when(ok)
            def _():
                pl.semaphore_signal(barrier, inc=1, device_id=(b + db, a + da), device_id_type=MESH)

    load = pltpu.make_async_copy(inv_hbm, inv_v, lsem)
    load.start()

    for d, (da, db) in enumerate(DIRS):

        @pl.when(jnp.logical_not(valid(d)))
        def _():
            for slot in range(ITERS + 1):
                if slot == 0:
                    rr, cc, kk = row0, col0, cor0
                else:
                    rr, cc, kk = row1.at[slot - 1], col1.at[slot - 1], cor1.at[slot - 1]
                if db == 0:
                    ref = rr.at[(da + 1) // 2]
                elif da == 0:
                    ref = cc.at[(db + 1) // 2]
                else:
                    ref = kk.at[(da + 1) + (db + 1) // 2]
                ref[...] = jnp.zeros(ref.shape, F32)

    step = 256
    numbering = wrow_ref[...]
    tall_numbering = jnp.transpose(jnp.broadcast_to(numbering, (LANES, LOCAL)))
    lane = lax.broadcasted_iota(jnp.int32, (LOCAL, LANES), 1)
    for c in range(0, LOCAL, LANES):
        perm_t[:, c : c + LANES] = jnp.where(lane + c == tall_numbering, 1.0, 0.0).astype(BF16)

    def hot(i, carry):
        off = pl.multiple_of(i * step, step)
        pos = lax.broadcasted_iota(jnp.int32, (step, LOCAL), 0) + off
        perm[pl.ds(off, step), :] = jnp.where(pos == numbering, 1.0, 0.0).astype(BF16)
        return carry

    lax.fori_loop(0, LOCAL // step, hot, 0)
    basis = basis_ref[0, 0]
    place = lax.rem(b, 3) * (MODES * N) + a * MODES
    line = lax.broadcasted_iota(jnp.int32, (LANES, LOCAL), 0) - place
    spread[...] = jnp.zeros(spread.shape, F32)
    for m in range(MODES):
        spread[...] = jnp.where(line == m, basis[m : m + 1], spread[...])
    b_high, b_low = split(jnp.transpose(spread[...]))
    packed = dot(perm[...], b_high) + dot(perm[...], b_low)
    x0[:, :, 2 * COLS :] = packed.reshape(ES, ES, LANES)
    classes = map_ref[...]
    conduct = jnp.zeros(classes.shape, F32)
    for k in range(class_ref.shape[0]):
        conduct = jnp.where(classes == k, class_ref[k], conduct)
    field[...] = jnp.zeros(field.shape, F32)
    field[0:CS, 0:CS] = conduct
    turned = jnp.transpose(field[...])[0:ES]
    lanes = lax.broadcasted_iota(jnp.int32, (ES, LANES), 1)
    last = lax.broadcasted_iota(jnp.int32, (CS, LANES), 1) == LANES - 1

    def fill(i, carry):
        u = OV + i
        column = jnp.sum(jnp.where(lanes == i, turned, 0.0), axis=1, keepdims=True)
        x0[u, OV : OV + CS, 0:COLS] = guess_ref[i]
        x0[u, OV : OV + CS, COLS : 2 * COLS] = rhs_ref[i]
        x0[u, OV : OV + CS, 2 * COLS :] = jnp.where(
            last, column[0:CS], x0[u, OV : OV + CS, 2 * COLS :]
        )
        return carry

    lax.fori_loop(0, CS, fill, 0)

    def strips(slot, src, rr, cc, cs, kk):
        copies = []
        for d, (da, db) in enumerate(DIRS):
            rows = pl.ds(hi if da > 0 else lo, H)
            if db == 0:
                part, dst = src.at[rows], rr.at[(1 - da) // 2]
            elif da == 0:
                part, dst = cs.at[(db + 1) // 2], cc.at[(1 - db) // 2]
            else:
                part = cs.at[(db + 1) // 2, pl.ds(0, H), pl.ds(ES - SUB if da > 0 else 0, SUB)]
                dst = kk.at[(1 - da) + (1 - db) // 2]
            copies.append(
                pltpu.make_async_remote_copy(
                    src_ref=part,
                    dst_ref=dst,
                    send_sem=ssem.at[slot, d],
                    recv_sem=rsem.at[slot, 7 - d],
                    device_id=(b + db, a + da),
                    device_id_type=MESH,
                )
            )
        return copies

    def pack(src, cs):
        def body(u, carry):
            for j in range(H):
                cs[0, j, pl.ds(u, 1), :] = src[u, lo + j : lo + j + 1, :]
                cs[1, j, pl.ds(u, 1), :] = src[u, hi + j : hi + j + 1, :]
            return carry

        lax.fori_loop(0, ES, body, 0)

    def send_strips(copies, dirs):
        for d in dirs:

            @pl.when(valid(d))
            def _():
                copies[d].start()

    def recv_strips(copies):
        for d in range(8):

            @pl.when(valid(d))
            def _():
                copies[7 - d].wait_recv()

    def done_strips(copies):
        for d in range(8):

            @pl.when(valid(d))
            def _():
                copies[d].wait_send()

    def unpack(dst, src, rr, cc, kk):
        def centre(i, carry):
            u = OV + i
            dst[u + 1, SUB : SUB + ES, :] = src[u]
            for j in range(H):
                p = SUB - 1 + j
                dst[u + 1, p : p + 1, :] = cc[0, j, pl.ds(u, 1), :]
                p = SUB + CS + OV + j
                dst[u + 1, p : p + 1, :] = cc[1, j, pl.ds(u, 1), :]
            return carry

        lax.fori_loop(0, CS, centre, 0)
        own = slice(OV, OV + CS)
        left, right = SUB - 1, SUB + CS + OV
        base = hi - (ES - SUB)
        for side, top in ((0, 0), (1, CS + H)):
            for j in range(H):
                dst[top + j, SUB + OV : SUB + OV + CS, :] = rr[side, j, own, :]
                row = (lo if side else base) + j
                for q in range(H):
                    at = left + q
                    dst[top + j, at : at + 1, :] = kk[2 * side, q, row : row + 1, :]
                    at = right + q
                    dst[top + j, at : at + 1, :] = kk[2 * side + 1, q, row : row + 1, :]

    def coarse_copy(slot, k, ref):
        _, target = other(k)
        return pltpu.make_async_remote_copy(
            src_ref=ref.at[a, b],
            dst_ref=ref.at[a, b],
            send_sem=gs.at[slot, k],
            recv_sem=gr.at[slot, me],
            device_id=target,
            device_id_type=MESH,
        )

    def coarse_send(slot, ref):
        def body(k, carry):
            coarse_copy(slot, k, ref).start()
            return carry

        lax.fori_loop(1, CHIPS, body, 0)

    def forward(slot, i, ref):
        return pltpu.make_async_remote_copy(
            src_ref=ref.at[2 * i + core],
            dst_ref=ref.at[2 * i + core],
            send_sem=fs.at[slot, i],
            recv_sem=fr.at[slot, i],
            device_id=(b, a + 1 - 2 * core),
            device_id_type=MESH,
        )

    def coarse_relay(slot, ref):
        def body(k, carry):
            idx, target = other(k)
            pltpu.make_async_remote_copy(
                src_ref=ref.at[a, b],
                dst_ref=ref.at[target[1], target[0]],
                send_sem=gs.at[slot, k],
                recv_sem=gr.at[slot, idx],
                device_id=target,
                device_id_type=MESH,
            ).wait_recv()
            return carry

        lax.fori_loop(1, CHIPS, body, 0)
        for i in range(HALF):
            forward(slot, i, ref).start()

    def coarse_recv(slot, ref):
        for i in range(HALF):
            pltpu.make_async_remote_copy(
                src_ref=ref.at[2 * i + core],
                dst_ref=ref.at[2 * i + 1 - core],
                send_sem=fs.at[slot, i],
                recv_sem=fr.at[slot, i],
                device_id=(b, a + 1 - 2 * core),
                device_id_type=MESH,
            ).wait_recv()

    def coarse_done(slot, ref):
        def body(k, carry):
            coarse_copy(slot, k, ref).wait_send()
            return carry

        lax.fori_loop(1, CHIPS, body, 0)
        for i in range(HALF):
            forward(slot, i, ref).wait_send()

    first = strips(0, x0, row0, col0, cs0, cor0)
    pack(x0, cs0)
    pl.semaphore_wait(barrier, count)
    send_strips(first, SIDES + ENDS)
    d0[...] = jnp.zeros(d0.shape, F32)
    wdeep[...] = jnp.zeros(wdeep.shape, F32)

    load.wait()

    def right_side_perm(i, carry):
        rows = pl.ds(pl.multiple_of(i * step, step), step)
        high, low = split(inv_v[rows, :])
        t_high[rows, :] = dot(high, perm_t[...]).astype(BF16)
        t_low[rows, :] = dot(low, perm_t[...]).astype(BF16)
        return carry

    lax.fori_loop(0, LOCAL // step, right_side_perm, 0)

    def left_side_perm(i, carry):
        rows = pl.ds(pl.multiple_of(i * step, step), step)
        l_high[rows, :] = dot(perm[rows, :], t_high[...]).astype(BF16)
        l_low[rows, :] = dot(perm[rows, :], t_low[...]).astype(BF16)
        return carry

    lax.fori_loop(0, LOCAL // step, left_side_perm, 0)
    line = lax.broadcasted_iota(jnp.int32, (2 * H * ES, LOCAL), 0)
    col = line >> int(math.log2(ES))
    col = jnp.where(col < H, col + lo, col - H + hi)
    pos = (line & (ES - 1)) * ES + col
    edge = jnp.where(pos == numbering, 1.0, 0.0).astype(BF16)
    e_high[...] = dot(edge, t_high[...]).astype(BF16)
    e_low[...] = dot(edge, t_low[...]).astype(BF16)
    m_high, m_low = split(jnp.concatenate([basis, jnp.zeros((SUB - MODES, LOCAL), F32)], axis=0))
    bw[0] = dot(m_high, perm_t[...]).astype(BF16)
    bw[1] = dot(m_low, perm_t[...]).astype(BF16)

    recv_strips(first)
    unpack(d0, x0, row0, col0, cor0)

    def modes(u, carry):
        value = d0[u, :, 2 * COLS :]
        high, low = split(value)
        rows = pl.ds(pl.multiple_of(u * DW, DW), DW)
        phi_high[rows, :] = high
        phi_low[rows, :] = low
        d0[u, :, 2 * COLS :] = jnp.broadcast_to(value[:, LANES - 1 : LANES], (DW, LANES))
        return carry

    lax.fori_loop(0, DH, modes, 0)
    col_pos = b * CS - OV + lax.broadcasted_iota(jnp.int32, (ES, LANES), 0)
    col_in = jnp.where((col_pos >= 0) & (col_pos < CS * W), 1.0, 0.0)

    def faces(u, carry):
        row_pos = a * CS - OV + u
        inside = jnp.where((row_pos >= 0) & (row_pos < CS * N), col_in, 0.0)
        cond = lambda du, dt: d0[u + 1 + du, SUB + dt : SUB + dt + ES, 2 * COLS :]
        own = cond(0, 0)
        half = 0.5 * inside
        weights[0, u] = REACTION * inside
        weights[1, u] = half * (own + cond(-1, 0))
        weights[2, u] = half * (own + cond(1, 0))
        weights[3, u] = half * (own + cond(0, -1))
        weights[4, u] = half * (own + cond(0, 1))
        return carry

    lax.fori_loop(0, ES, faces, 0)

    def operator(ref, u):
        parts = []
        for c in range(0, COLS, LANES):
            at = lambda du, dt: ref[u + 1 + du, SUB + dt : SUB + dt + ES, c : c + LANES]
            mid = at(0, 0)
            parts.append(
                weights[0, u] * mid
                + weights[1, u] * (mid - at(-1, 0))
                + weights[2, u] * (mid - at(1, 0))
                + weights[3, u] * (mid - at(0, -1))
                + weights[4, u] * (mid - at(0, 1))
            )
        return jnp.concatenate(parts, axis=1)

    def set_x(u, value):
        high, low = split(value)
        rows = pl.ds(pl.multiple_of(u * ES, ES), ES)
        x_high[rows, :] = high
        x_low[rows, :] = low

    def first_residual(u, carry):
        inside = jnp.where(weights[0, u] > 0.0, 1.0, 0.0)
        inside = jnp.concatenate([inside] * (COLS // LANES), axis=1)
        right = d0[u + 1, SUB : SUB + ES, COLS : 2 * COLS]
        value = right * inside - operator(d0, u)
        res[u] = value
        set_x(u, value)
        return carry

    lax.fori_loop(0, ES, first_residual, 0)

    def start_sol(i, carry):
        sol[i] = d0[OV + i + 1, SUB : SUB + ES, 0:COLS]
        return carry

    lax.fori_loop(0, CS, start_sol, 0)

    def coarse_rows():
        return dot3(bw[0], bw[1], x_high[...], x_low[...])

    sub_pos = lax.broadcasted_iota(jnp.int32, (SUB, COLS), 0)
    pending = []
    numer = denom = None
    for it in range(ITERS + 1):
        ref = g0 if it == 0 else g.at[it - 1]
        if it == 0:
            ref[a, b] = jnp.zeros((ref.shape[2], COLS), F32)
            ref[a, b, 0:SUB, :] = coarse_rows()
            run = MODES * W
            for i in range(MODES * N):
                line, at = divmod(i * run, COLS)
                ref[a, b, MODES + line, at : at + run] = coarse_ref[i]
        else:
            rows = coarse_rows() if it < ITERS else jnp.zeros((SUB, COLS), F32)
            rows = jnp.where(sub_pos == MODES, numer, rows)
            rows = jnp.where(sub_pos == MODES + 1, denom, rows)
            ref[a, b] = rows
        coarse_send(it, ref)
        if it == ITERS:
            own = pl.ds(OV, CS)
            pairs = (
                (sol, sol_out),
                (deep.at[pl.ds(OV + 1, CS), pl.ds(SUB, ES)], dir_out),
                (res.at[own], res_out),
                (img.at[own], img_out),
            )
            writes = [
                pltpu.make_async_copy(src, dst, osem.at[n]) for n, (src, dst) in enumerate(pairs)
            ]
            for copy in writes:
                copy.start()
        if it < ITERS:
            value = dot3(e_high[...], e_low[...], x_high[...], x_low[...])
            cs1[it] = value.reshape(2, H, ES, COLS)
            copies = strips(it + 1, z.at[it], row1.at[it], col1.at[it], cs1.at[it], cor1.at[it])
            send_strips(copies, SIDES)

            def solve(i, carry):
                rows = pl.ds(pl.multiple_of(i * step, step), step)
                value = dot3(l_high[rows, :], l_low[rows, :], x_high[...], x_low[...])
                z[it, pl.ds(i * (step // ES), step // ES)] = value.reshape(step // ES, ES, COLS)
                return carry

            lax.fori_loop(0, LOCAL // step, solve, 0)
            send_strips(copies, ENDS)
            pending.append(copies)
        coarse_relay(it, ref)
        coarse_recv(it, ref)
        if it == 0:
            per = COLS // (4 * W)
            wide_cols = MODES * W
            group = MODES * N
            piece = lax.broadcasted_iota(jnp.int32, (group, COLS), 0) & (per - 1)
            lane = lax.broadcasted_iota(jnp.int32, (group, COLS), 1)
            keep = (lane >> int(math.log2(wide_cols))) == piece
            width = N * W * SUB
            j = lax.broadcasted_iota(jnp.int32, (COLS, width), 0) & (wide_cols - 1)
            c = lax.broadcasted_iota(jnp.int32, (COLS, width), 1)
            total_high = total_low = None
            for a2 in range(N):
                blocks = []
                for third in range(3):
                    db = lax.rem(third - b + 1 + 3 * W, 3) - 1
                    at = jnp.clip(b + db, 0, W - 1)
                    raw = ref[a2, at, MODES : MODES + KR, :]
                    tall = jnp.concatenate(
                        [jnp.broadcast_to(raw[r : r + 1], (per, COLS)) for r in range(KR)], axis=0
                    )
                    blocks.append(jnp.where(keep, tall, 0.0))
                blocks.append(jnp.zeros((LANES - 3 * group, COLS), F32))
                high, low = split(jnp.concatenate(blocks, axis=0))
                fold = c == a2 * (W * SUB) + (j >> 2) * SUB + (j & 3)
                fold = jnp.where(fold, 1.0, 0.0).astype(BF16)
                th, tl = dot(high, fold), dot(low, fold)
                total_high = th if total_high is None else total_high + th
                total_low = tl if total_low is None else total_low + tl
            kmat[0] = total_high.astype(BF16)
            kmat[1] = total_low.astype(BF16)
        else:
            total = jnp.sum(ref[...].reshape(N * W, SUB, COLS), axis=0)
            size = total[MODES : MODES + 1] / total[MODES + 1 : MODES + 2]
        if it == ITERS:
            break
        g_high, g_low = split(ref[:, :, 0:SUB, :].reshape(N * W * SUB, COLS))
        s_high, s_low = split(dot3(kmat[0], kmat[1], g_high, g_low))
        recv_strips(copies)
        unpack(wdeep, z.at[it], row1.at[it], col1.at[it], cor1.at[it])

        if it > 0:

            def advance(i, carry):
                u = OV + i
                sol[i] = sol[i] + size * deep[u + 1, SUB : SUB + ES, :]
                res[u] = res[u] - size * img[u]
                return carry

            lax.fori_loop(0, CS, advance, 0)
        chunk = DH // 2

        def coarse_part(i, carry):
            rows = pl.ds(pl.multiple_of(i * chunk * DW, chunk * DW), chunk * DW)
            value = dot3(phi_high[rows, :], phi_low[rows, :], s_high, s_low)
            tall = pl.ds(i * chunk, chunk)
            value = value.reshape(chunk, DW, COLS) + wdeep[tall]
            if it == 0:
                deep[tall] = value
            else:
                deep[tall] = deep[tall] - size * value
            return carry

        lax.fori_loop(0, 2, coarse_part, 0)

        def apply(u, carry):
            top, bottom = carry
            value = operator(deep, u)
            img[u] = value
            if it < ITERS - 1:
                set_x(u, value)
            own = jnp.where((u >= OV) & (u < OV + CS), value, 0.0)
            return top + res[u] * own, bottom + value * own

        nothing = jnp.zeros((ES, COLS), F32)
        top, bottom = lax.fori_loop(0, ES, apply, (nothing, nothing))
        col = lax.broadcasted_iota(jnp.int32, (ES, COLS), 0)
        mine = (col >= OV) & (col < OV + CS)
        numer = jnp.sum(jnp.where(mine, top, 0.0), axis=0, keepdims=True)
        denom = jnp.sum(jnp.where(mine, bottom, 0.0), axis=0, keepdims=True)

    done_strips(first)
    for copies in pending:
        done_strips(copies)
    size_out[...] = jnp.broadcast_to(size, (SUB, COLS))
    for copy in writes:
        copy.wait()
    for it in range(ITERS + 1):
        coarse_done(it, g0 if it == 0 else g.at[it - 1])


def finish(OV, CS, sol, direction, res, image, size, sol_out, res_out):
    step = size[0:1]
    for i in range(sol.shape[0]):
        sol_out[i] = (sol[i] + step * direction[i])[OV : OV + CS]
        res_out[i] = (res[i] - step * image[i])[OV : OV + CS]


def local(
    N,
    W,
    right_side,
    initial_guess,
    class_map,
    class_conductivity,
    window_index,
    local_inverse,
    coarse_basis,
    coarse_inverse,
):
    CS, _, COLS = right_side.shape
    MODES, LOCAL = coarse_basis.shape[2:]
    ES = math.isqrt(LOCAL)
    OV = (ES - CS) // 2
    H = OV + 1
    DW, DH = ES + 2 * SUB, ES + 2
    KR = coarse_inverse.size // COLS
    R0 = -(-(MODES + KR) // SUB) * SUB
    CHIPS = N * W // 2
    vmem = pl.BlockSpec(memory_space=pltpu.VMEM)
    big = 2 * COLS + LANES
    scratch = [
        pltpu.VMEM((LOCAL, LOCAL), F32),
        pltpu.VMEM((LOCAL, LOCAL), BF16),
        pltpu.VMEM((LOCAL, LOCAL), BF16),
        pltpu.VMEM((LOCAL, LOCAL), BF16),
        pltpu.VMEM((LOCAL, LOCAL), BF16),
        pltpu.VMEM((LOCAL, LOCAL), BF16),
        pltpu.VMEM((LOCAL, LOCAL), BF16),
        pltpu.VMEM((ES, ES, big), F32),
        pltpu.VMEM((DH, DW, big), F32),
        pltpu.VMEM((5, ES, ES, LANES), F32),
        pltpu.VMEM((DH * DW, LANES), BF16),
        pltpu.VMEM((DH * DW, LANES), BF16),
        pltpu.VMEM((2, SUB, LOCAL), BF16),
        pltpu.VMEM((LOCAL, COLS), BF16),
        pltpu.VMEM((LOCAL, COLS), BF16),
        pltpu.VMEM((ES, ES, COLS), F32),
        pltpu.VMEM((CS, ES, COLS), F32),
        pltpu.VMEM((ES, ES, COLS), F32),
        pltpu.VMEM((DH, DW, COLS), F32),
        pltpu.VMEM((DH, DW, COLS), F32),
        pltpu.VMEM((ITERS, ES, ES, COLS), F32),
        pltpu.VMEM((2, LANES, N * W * SUB), BF16),
        pltpu.VMEM((N, W, R0, COLS), F32),
        pltpu.VMEM((ITERS, N, W, SUB, COLS), F32),
        pltpu.VMEM((2, H, ES, big), F32),
        pltpu.VMEM((2, H, ES, big), F32),
        pltpu.VMEM((2, H, ES, big), F32),
        pltpu.VMEM((4, H, SUB, big), F32),
        pltpu.VMEM((ITERS, 2, H, ES, COLS), F32),
        pltpu.VMEM((ITERS, 2, H, ES, COLS), F32),
        pltpu.VMEM((ITERS, 2, H, ES, COLS), F32),
        pltpu.VMEM((ITERS, 4, H, SUB, COLS), F32),
        pltpu.SemaphoreType.DMA((ITERS + 1, 8)),
        pltpu.SemaphoreType.DMA((ITERS + 1, 8)),
        pltpu.SemaphoreType.DMA((ITERS + 1, CHIPS)),
        pltpu.SemaphoreType.DMA((ITERS + 1, CHIPS)),
        pltpu.SemaphoreType.DMA((ITERS + 1, N // 2)),
        pltpu.SemaphoreType.DMA((ITERS + 1, N // 2)),
        pltpu.SemaphoreType.DMA,
        pltpu.SemaphoreType.DMA((4,)),
        pltpu.VMEM((LANES, LANES), F32),
        pltpu.VMEM((LANES, LOCAL), F32),
        pltpu.VMEM((2 * H * ES, LOCAL), BF16),
        pltpu.VMEM((2 * H * ES, LOCAL), BF16),
    ]
    out = jax.ShapeDtypeStruct((CS, ES, COLS), F32)
    anywhere = pl.BlockSpec(memory_space=pl.ANY)
    smem = pl.BlockSpec(memory_space=pltpu.SMEM)
    *fields, size = pl.pallas_call(
        functools.partial(kernel, (N, W, ES, OV, CS, COLS, MODES, KR)),
        out_shape=(out,) * 4 + (jax.ShapeDtypeStruct((SUB, COLS), F32),),
        in_specs=[vmem] * 3 + [smem, vmem, anywhere] + [vmem] * 2,
        out_specs=(anywhere,) * 4 + (vmem,),
        scratch_shapes=scratch,
        compiler_params=pltpu.CompilerParams(
            collective_id=0, has_side_effects=True, vmem_limit_bytes=67043328
        ),
        name="schwarz",
    )(
        right_side,
        initial_guess,
        class_map,
        class_conductivity,
        window_index[0],
        local_inverse[0, 0],
        coarse_basis,
        coarse_inverse,
    )
    block = CS // 4
    part = pl.BlockSpec((block, ES, COLS), lambda i: (i, 0, 0))
    done = pl.BlockSpec((block, CS, COLS), lambda i: (i, 0, 0))
    return pl.pallas_call(
        functools.partial(finish, OV, CS),
        grid=(CS // block,),
        out_shape=(jax.ShapeDtypeStruct(right_side.shape, F32),) * 2,
        in_specs=[part] * 4 + [pl.BlockSpec((SUB, COLS), lambda i: (0, 0))],
        out_specs=(done, done),
        name="finish",
    )(*fields, size)


def solution(mesh):
    in_specs = (
        P("narrow", "wide", None),
        P("narrow", "wide", None),
        P("narrow", "wide"),
        P(),
        P("narrow", "wide", None),
        P("narrow", "wide", None, None),
        P("narrow", "wide", None, None),
        P("wide", "narrow"),
    )
    out_specs = (P("narrow", "wide", None), P("narrow", "wide", None))
    body = functools.partial(local, mesh.shape["narrow"], mesh.shape["wide"])
    return jax.shard_map(body, mesh=mesh, in_specs=in_specs, out_specs=out_specs, check_vma=False)
```

```python
import functools
import math

import jax
import jax.numpy as jnp
from jax import lax
from jax.experimental import pallas as pl
from jax.experimental.pallas import tpu as pltpu
from jax.sharding import PartitionSpec as P

ITERS = 3
REACTION = 0.01
LANES = 128
SUB = 8
F32 = jnp.float32
BF16 = jnp.bfloat16
MESH = pl.DeviceIdType.MESH
DIRS = ((-1, -1), (-1, 0), (-1, 1), (0, -1), (0, 1), (1, -1), (1, 0), (1, 1))

SIDES = (3, 4, 0, 2, 5, 7)
ENDS = (1, 6)


def split(value):
    high = value.astype(BF16)
    return high, (value - high.astype(F32)).astype(BF16)


def dot(left, right):
    return jnp.dot(left, right, preferred_element_type=F32)


def dot3(left_high, left_low, right_high, right_low):
    return dot(left_high, right_high) + (dot(left_low, right_high) + dot(left_high, right_low))


def kernel(
    cfg,
    rhs_ref,
    guess_ref,
    map_ref,
    class_ref,
    wrow_ref,
    inv_hbm,
    basis_ref,
    coarse_ref,
    sol_out,
    dir_out,
    res_out,
    img_out,
    size_out,
    inv_v,
    perm,
    perm_t,
    t_high,
    t_low,
    l_high,
    l_low,
    x0,
    d0,
    weights,
    phi_high,
    phi_low,
    bw,
    x_high,
    x_low,
    res,
    sol,
    img,
    deep,
    wdeep,
    z,
    kmat,
    g0,
    g,
    row0,
    col0,
    cs0,
    cor0,
    row1,
    col1,
    cs1,
    cor1,
    ssem,
    rsem,
    gs,
    gr,
    fs,
    fr,
    lsem,
    osem,
    field,
    spread,
    e_high,
    e_low,
):
    N, W, ES, OV, CS, COLS, MODES, KR = cfg
    H = OV + 1
    lo, hi = OV, OV + CS - H
    LOCAL = ES * ES
    DW = ES + 2 * SUB
    DH = ES + 2
    HALF = N // 2
    CHIPS = HALF * W
    a = lax.axis_index("narrow")
    b = lax.axis_index("wide")
    core = lax.rem(a, 2)
    me = (a // 2) * W + b

    def other(k):
        idx = lax.rem(me + k, CHIPS)
        return idx, (lax.rem(idx, W), 2 * (idx // W) + core)

    def valid(d):
        da, db = DIRS[d]
        return (a + da >= 0) & (a + da < N) & (b + db >= 0) & (b + db < W)

    barrier = pltpu.get_barrier_semaphore()

    def greet(k, carry):
        pl.semaphore_signal(barrier, inc=1, device_id=other(k)[1], device_id_type=MESH)
        return carry

    lax.fori_loop(1, CHIPS, greet, 0)
    count = CHIPS - 1
    for d, (da, db) in enumerate(DIRS):
        if da != 0:
            ok = valid(d)
            count = count + ok.astype(jnp.int32)

            @pl.when(ok)
            def _():
                pl.semaphore_signal(barrier, inc=1, device_id=(b + db, a + da), device_id_type=MESH)

    load = pltpu.make_async_copy(inv_hbm, inv_v, lsem)
    load.start()

    for d, (da, db) in enumerate(DIRS):

        @pl.when(jnp.logical_not(valid(d)))
        def _():
            for slot in range(ITERS + 1):
                if slot == 0:
                    rr, cc, kk = row0, col0, cor0
                else:
                    rr, cc, kk = row1.at[slot - 1], col1.at[slot - 1], cor1.at[slot - 1]
                if db == 0:
                    ref = rr.at[(da + 1) // 2]
                elif da == 0:
                    ref = cc.at[(db + 1) // 2]
                else:
                    ref = kk.at[(da + 1) + (db + 1) // 2]
                ref[...] = jnp.zeros(ref.shape, F32)

    step = 256
    numbering = wrow_ref[...]
    tall_numbering = jnp.transpose(jnp.broadcast_to(numbering, (LANES, LOCAL)))
    lane = lax.broadcasted_iota(jnp.int32, (LOCAL, LANES), 1)
    for c in range(0, LOCAL, LANES):
        perm_t[:, c : c + LANES] = jnp.where(lane + c == tall_numbering, 1.0, 0.0).astype(BF16)

    def hot(i, carry):
        off = pl.multiple_of(i * step, step)
        pos = lax.broadcasted_iota(jnp.int32, (step, LOCAL), 0) + off
        perm[pl.ds(off, step), :] = jnp.where(pos == numbering, 1.0, 0.0).astype(BF16)
        return carry

    lax.fori_loop(0, LOCAL // step, hot, 0)
    basis = basis_ref[0, 0]
    place = lax.rem(b, 3) * (MODES * N) + a * MODES
    line = lax.broadcasted_iota(jnp.int32, (LANES, LOCAL), 0) - place
    spread[...] = jnp.zeros(spread.shape, F32)
    for m in range(MODES):
        spread[...] = jnp.where(line == m, basis[m : m + 1], spread[...])
    b_high, b_low = split(jnp.transpose(spread[...]))
    packed = dot(perm[...], b_high) + dot(perm[...], b_low)
    x0[:, :, 2 * COLS :] = packed.reshape(ES, ES, LANES)
    classes = map_ref[...]
    conduct = jnp.zeros(classes.shape, F32)
    for k in range(class_ref.shape[0]):
        conduct = jnp.where(classes == k, class_ref[k], conduct)
    field[...] = jnp.zeros(field.shape, F32)
    field[0:CS, 0:CS] = conduct
    turned = jnp.transpose(field[...])[0:ES]
    lanes = lax.broadcasted_iota(jnp.int32, (ES, LANES), 1)
    last = lax.broadcasted_iota(jnp.int32, (CS, LANES), 1) == LANES - 1

    def fill(i, carry):
        u = OV + i
        column = jnp.sum(jnp.where(lanes == i, turned, 0.0), axis=1, keepdims=True)
        x0[u, OV : OV + CS, 0:COLS] = guess_ref[i]
        x0[u, OV : OV + CS, COLS : 2 * COLS] = rhs_ref[i]
        x0[u, OV : OV + CS, 2 * COLS :] = jnp.where(
            last, column[0:CS], x0[u, OV : OV + CS, 2 * COLS :]
        )
        return carry

    lax.fori_loop(0, CS, fill, 0)

    def strips(slot, src, rr, cc, cs, kk):
        copies = []
        for d, (da, db) in enumerate(DIRS):
            rows = pl.ds(hi if da > 0 else lo, H)
            if db == 0:
                part, dst = src.at[rows], rr.at[(1 - da) // 2]
            elif da == 0:
                part, dst = cs.at[(db + 1) // 2], cc.at[(1 - db) // 2]
            else:
                part = cs.at[(db + 1) // 2, pl.ds(0, H), pl.ds(ES - SUB if da > 0 else 0, SUB)]
                dst = kk.at[(1 - da) + (1 - db) // 2]
            copies.append(
                pltpu.make_async_remote_copy(
                    src_ref=part,
                    dst_ref=dst,
                    send_sem=ssem.at[slot, d],
                    recv_sem=rsem.at[slot, 7 - d],
                    device_id=(b + db, a + da),
                    device_id_type=MESH,
                )
            )
        return copies

    def pack(src, cs):
        def body(u, carry):
            for j in range(H):
                cs[0, j, pl.ds(u, 1), :] = src[u, lo + j : lo + j + 1, :]
                cs[1, j, pl.ds(u, 1), :] = src[u, hi + j : hi + j + 1, :]
            return carry

        lax.fori_loop(0, ES, body, 0)

    def send_strips(copies, dirs):
        for d in dirs:

            @pl.when(valid(d))
            def _():
                copies[d].start()

    def recv_strips(copies):
        for d in range(8):

            @pl.when(valid(d))
            def _():
                copies[7 - d].wait_recv()

    def done_strips(copies):
        for d in range(8):

            @pl.when(valid(d))
            def _():
                copies[d].wait_send()

    def centre(dst, src):
        def body(i, carry):
            u = OV + i
            dst[u + 1, SUB : SUB + ES, :] = src[u]
            return carry

        lax.fori_loop(0, CS, body, 0)

    def unpack(dst, rr, cc, kk):
        def sides(i, carry):
            u = OV + i
            for j in range(H):
                p = SUB - 1 + j
                dst[u + 1, p : p + 1, :] = cc[0, j, pl.ds(u, 1), :]
                p = SUB + CS + OV + j
                dst[u + 1, p : p + 1, :] = cc[1, j, pl.ds(u, 1), :]
            return carry

        lax.fori_loop(0, CS, sides, 0)
        own = slice(OV, OV + CS)
        left, right = SUB - 1, SUB + CS + OV
        base = hi - (ES - SUB)
        for side, top in ((0, 0), (1, CS + H)):
            for j in range(H):
                dst[top + j, SUB + OV : SUB + OV + CS, :] = rr[side, j, own, :]
                row = (lo if side else base) + j
                for q in range(H):
                    at = left + q
                    dst[top + j, at : at + 1, :] = kk[2 * side, q, row : row + 1, :]
                    at = right + q
                    dst[top + j, at : at + 1, :] = kk[2 * side + 1, q, row : row + 1, :]

    def coarse_copy(slot, k, ref):
        _, target = other(k)
        return pltpu.make_async_remote_copy(
            src_ref=ref.at[a, b],
            dst_ref=ref.at[a, b],
            send_sem=gs.at[slot, k],
            recv_sem=gr.at[slot, me],
            device_id=target,
            device_id_type=MESH,
        )

    def coarse_send(slot, ref):
        def body(k, carry):
            coarse_copy(slot, k, ref).start()
            return carry

        lax.fori_loop(1, CHIPS, body, 0)

    def forward(slot, i, ref):
        return pltpu.make_async_remote_copy(
            src_ref=ref.at[2 * i + core],
            dst_ref=ref.at[2 * i + core],
            send_sem=fs.at[slot, i],
            recv_sem=fr.at[slot, i],
            device_id=(b, a + 1 - 2 * core),
            device_id_type=MESH,
        )

    def coarse_relay(slot, ref):
        def body(k, carry):
            idx, target = other(k)
            pltpu.make_async_remote_copy(
                src_ref=ref.at[a, b],
                dst_ref=ref.at[target[1], target[0]],
                send_sem=gs.at[slot, k],
                recv_sem=gr.at[slot, idx],
                device_id=target,
                device_id_type=MESH,
            ).wait_recv()
            return carry

        lax.fori_loop(1, CHIPS, body, 0)
        for i in range(HALF):
            forward(slot, i, ref).start()

    def coarse_recv(slot, ref):
        for i in range(HALF):
            pltpu.make_async_remote_copy(
                src_ref=ref.at[2 * i + core],
                dst_ref=ref.at[2 * i + 1 - core],
                send_sem=fs.at[slot, i],
                recv_sem=fr.at[slot, i],
                device_id=(b, a + 1 - 2 * core),
                device_id_type=MESH,
            ).wait_recv()

    def coarse_done(slot, ref):
        def body(k, carry):
            coarse_copy(slot, k, ref).wait_send()
            return carry

        lax.fori_loop(1, CHIPS, body, 0)
        for i in range(HALF):
            forward(slot, i, ref).wait_send()

    first = strips(0, x0, row0, col0, cs0, cor0)
    pack(x0, cs0)
    pl.semaphore_wait(barrier, count)
    send_strips(first, SIDES + ENDS)
    d0[...] = jnp.zeros(d0.shape, F32)
    wdeep[...] = jnp.zeros(wdeep.shape, F32)

    load.wait()

    def right_side_perm(i, carry):
        rows = pl.ds(pl.multiple_of(i * step, step), step)
        high, low = split(inv_v[rows, :])
        t_high[rows, :] = dot(high, perm_t[...]).astype(BF16)
        t_low[rows, :] = dot(low, perm_t[...]).astype(BF16)
        return carry

    lax.fori_loop(0, LOCAL // step, right_side_perm, 0)

    def left_side_perm(i, carry):
        rows = pl.ds(pl.multiple_of(i * step, step), step)
        l_high[rows, :] = dot(perm[rows, :], t_high[...]).astype(BF16)
        l_low[rows, :] = dot(perm[rows, :], t_low[...]).astype(BF16)
        return carry

    lax.fori_loop(0, LOCAL // step, left_side_perm, 0)
    line = lax.broadcasted_iota(jnp.int32, (2 * H * ES, LOCAL), 0)
    col = line >> int(math.log2(ES))
    col = jnp.where(col < H, col + lo, col - H + hi)
    pos = (line & (ES - 1)) * ES + col
    edge = jnp.where(pos == numbering, 1.0, 0.0).astype(BF16)
    e_high[...] = dot(edge, t_high[...]).astype(BF16)
    e_low[...] = dot(edge, t_low[...]).astype(BF16)
    m_high, m_low = split(jnp.concatenate([basis, jnp.zeros((SUB - MODES, LOCAL), F32)], axis=0))
    bw[0] = dot(m_high, perm_t[...]).astype(BF16)
    bw[1] = dot(m_low, perm_t[...]).astype(BF16)

    centre(d0, x0)

    def start_sol(i, carry):
        sol[i] = x0[OV + i, :, 0:COLS]
        return carry

    lax.fori_loop(0, CS, start_sol, 0)
    recv_strips(first)
    unpack(d0, row0, col0, cor0)

    def modes(u, carry):
        value = d0[u, :, 2 * COLS :]
        high, low = split(value)
        rows = pl.ds(pl.multiple_of(u * DW, DW), DW)
        phi_high[rows, :] = high
        phi_low[rows, :] = low
        d0[u, :, 2 * COLS :] = jnp.broadcast_to(value[:, LANES - 1 : LANES], (DW, LANES))
        return carry

    lax.fori_loop(0, DH, modes, 0)
    col_pos = b * CS - OV + lax.broadcasted_iota(jnp.int32, (ES, LANES), 0)
    col_in = jnp.where((col_pos >= 0) & (col_pos < CS * W), 1.0, 0.0)

    def faces(u, carry):
        row_pos = a * CS - OV + u
        inside = jnp.where((row_pos >= 0) & (row_pos < CS * N), col_in, 0.0)
        cond = lambda du, dt: d0[u + 1 + du, SUB + dt : SUB + dt + ES, 2 * COLS :]
        own = cond(0, 0)
        half = 0.5 * inside
        weights[0, u] = REACTION * inside
        weights[1, u] = half * (own + cond(-1, 0))
        weights[2, u] = half * (own + cond(1, 0))
        weights[3, u] = half * (own + cond(0, -1))
        weights[4, u] = half * (own + cond(0, 1))
        return carry

    lax.fori_loop(0, ES, faces, 0)

    def operator(ref, u):
        parts = []
        for c in range(0, COLS, LANES):
            at = lambda du, dt: ref[u + 1 + du, SUB + dt : SUB + dt + ES, c : c + LANES]
            mid = at(0, 0)
            parts.append(
                weights[0, u] * mid
                + weights[1, u] * (mid - at(-1, 0))
                + weights[2, u] * (mid - at(1, 0))
                + weights[3, u] * (mid - at(0, -1))
                + weights[4, u] * (mid - at(0, 1))
            )
        return jnp.concatenate(parts, axis=1)

    def set_x(u, value):
        high, low = split(value)
        rows = pl.ds(pl.multiple_of(u * ES, ES), ES)
        x_high[rows, :] = high
        x_low[rows, :] = low

    def first_residual(u, carry):
        inside = jnp.where(weights[0, u] > 0.0, 1.0, 0.0)
        inside = jnp.concatenate([inside] * (COLS // LANES), axis=1)
        right = d0[u + 1, SUB : SUB + ES, COLS : 2 * COLS]
        value = right * inside - operator(d0, u)
        res[u] = value
        set_x(u, value)
        return carry

    lax.fori_loop(0, ES, first_residual, 0)

    def coarse_rows():
        return dot3(bw[0], bw[1], x_high[...], x_low[...])

    sub_pos = lax.broadcasted_iota(jnp.int32, (SUB, COLS), 0)
    pending = []
    numer = denom = None
    for it in range(ITERS + 1):
        ref = g0 if it == 0 else g.at[it - 1]
        if it == 0:
            ref[a, b] = jnp.zeros((ref.shape[2], COLS), F32)
            ref[a, b, 0:SUB, :] = coarse_rows()
            run = MODES * W
            for i in range(MODES * N):
                line, at = divmod(i * run, COLS)
                ref[a, b, MODES + line, at : at + run] = coarse_ref[i]
        else:
            rows = coarse_rows() if it < ITERS else jnp.zeros((SUB, COLS), F32)
            rows = jnp.where(sub_pos == MODES, numer, rows)
            rows = jnp.where(sub_pos == MODES + 1, denom, rows)
            ref[a, b] = rows
        coarse_send(it, ref)
        if it == ITERS:
            own = pl.ds(OV, CS)
            pairs = (
                (sol, sol_out),
                (deep.at[pl.ds(OV + 1, CS), pl.ds(SUB, ES)], dir_out),
                (res.at[own], res_out),
                (img.at[own], img_out),
            )
            writes = [
                pltpu.make_async_copy(src, dst, osem.at[n]) for n, (src, dst) in enumerate(pairs)
            ]
            for copy in writes:
                copy.start()
        if it < ITERS:
            value = dot3(e_high[...], e_low[...], x_high[...], x_low[...])
            cs1[it] = value.reshape(2, H, ES, COLS)
            copies = strips(it + 1, z.at[it], row1.at[it], col1.at[it], cs1.at[it], cor1.at[it])
            send_strips(copies, SIDES)

            def solve(i, carry):
                rows = pl.ds(pl.multiple_of(i * step, step), step)
                value = dot3(l_high[rows, :], l_low[rows, :], x_high[...], x_low[...])
                z[it, pl.ds(i * (step // ES), step // ES)] = value.reshape(step // ES, ES, COLS)
                return carry

            lax.fori_loop(0, LOCAL // step, solve, 0)
            send_strips(copies, ENDS)
            centre(wdeep, z.at[it])
            pending.append(copies)
        coarse_relay(it, ref)
        coarse_recv(it, ref)
        if it == 0:
            per = COLS // (4 * W)
            wide_cols = MODES * W
            group = MODES * N
            piece = lax.broadcasted_iota(jnp.int32, (group, COLS), 0) & (per - 1)
            lane = lax.broadcasted_iota(jnp.int32, (group, COLS), 1)
            keep = (lane >> int(math.log2(wide_cols))) == piece
            width = N * W * SUB
            j = lax.broadcasted_iota(jnp.int32, (COLS, width), 0) & (wide_cols - 1)
            c = lax.broadcasted_iota(jnp.int32, (COLS, width), 1)
            total_high = total_low = None
            for a2 in range(N):
                blocks = []
                for third in range(3):
                    db = lax.rem(third - b + 1 + 3 * W, 3) - 1
                    at = jnp.clip(b + db, 0, W - 1)
                    raw = ref[a2, at, MODES : MODES + KR, :]
                    tall = jnp.concatenate(
                        [jnp.broadcast_to(raw[r : r + 1], (per, COLS)) for r in range(KR)], axis=0
                    )
                    blocks.append(jnp.where(keep, tall, 0.0))
                blocks.append(jnp.zeros((LANES - 3 * group, COLS), F32))
                high, low = split(jnp.concatenate(blocks, axis=0))
                fold = c == a2 * (W * SUB) + (j >> 2) * SUB + (j & 3)
                fold = jnp.where(fold, 1.0, 0.0).astype(BF16)
                th, tl = dot(high, fold), dot(low, fold)
                total_high = th if total_high is None else total_high + th
                total_low = tl if total_low is None else total_low + tl
            kmat[0] = total_high.astype(BF16)
            kmat[1] = total_low.astype(BF16)
        else:
            total = jnp.sum(ref[...].reshape(N * W, SUB, COLS), axis=0)
            size = total[MODES : MODES + 1] / total[MODES + 1 : MODES + 2]
        if it == ITERS:
            break
        g_high, g_low = split(ref[:, :, 0:SUB, :].reshape(N * W * SUB, COLS))
        s_high, s_low = split(dot3(kmat[0], kmat[1], g_high, g_low))
        if it > 0:

            def advance(i, carry):
                u = OV + i
                sol[i] = sol[i] + size * deep[u + 1, SUB : SUB + ES, :]
                res[u] = res[u] - size * img[u]
                return carry

            lax.fori_loop(0, CS, advance, 0)
        recv_strips(copies)
        unpack(wdeep, row1.at[it], col1.at[it], cor1.at[it])
        chunk = DH // 2

        def coarse_part(i, carry):
            rows = pl.ds(pl.multiple_of(i * chunk * DW, chunk * DW), chunk * DW)
            value = dot3(phi_high[rows, :], phi_low[rows, :], s_high, s_low)
            tall = pl.ds(i * chunk, chunk)
            value = value.reshape(chunk, DW, COLS) + wdeep[tall]
            if it == 0:
                deep[tall] = value
            else:
                deep[tall] = deep[tall] - size * value
            return carry

        lax.fori_loop(0, 2, coarse_part, 0)

        def apply(u, carry):
            top, bottom = carry
            value = operator(deep, u)
            img[u] = value
            if it < ITERS - 1:
                set_x(u, value)
            own = jnp.where((u >= OV) & (u < OV + CS), value, 0.0)
            return top + res[u] * own, bottom + value * own

        nothing = jnp.zeros((ES, COLS), F32)
        top, bottom = lax.fori_loop(0, ES, apply, (nothing, nothing))
        col = lax.broadcasted_iota(jnp.int32, (ES, COLS), 0)
        mine = (col >= OV) & (col < OV + CS)
        numer = jnp.sum(jnp.where(mine, top, 0.0), axis=0, keepdims=True)
        denom = jnp.sum(jnp.where(mine, bottom, 0.0), axis=0, keepdims=True)

    done_strips(first)
    for copies in pending:
        done_strips(copies)
    size_out[...] = jnp.broadcast_to(size, (SUB, COLS))
    for copy in writes:
        copy.wait()
    for it in range(ITERS + 1):
        coarse_done(it, g0 if it == 0 else g.at[it - 1])


def finish(OV, CS, sol, direction, res, image, size, sol_out, res_out):
    step = size[0:1]
    for i in range(sol.shape[0]):
        sol_out[i] = (sol[i] + step * direction[i])[OV : OV + CS]
        res_out[i] = (res[i] - step * image[i])[OV : OV + CS]


def local(
    N,
    W,
    right_side,
    initial_guess,
    class_map,
    class_conductivity,
    window_index,
    local_inverse,
    coarse_basis,
    coarse_inverse,
):
    CS, _, COLS = right_side.shape
    MODES, LOCAL = coarse_basis.shape[2:]
    ES = math.isqrt(LOCAL)
    OV = (ES - CS) // 2
    H = OV + 1
    DW, DH = ES + 2 * SUB, ES + 2
    KR = coarse_inverse.size // COLS
    R0 = -(-(MODES + KR) // SUB) * SUB
    CHIPS = N * W // 2
    vmem = pl.BlockSpec(memory_space=pltpu.VMEM)
    big = 2 * COLS + LANES
    scratch = [
        pltpu.VMEM((LOCAL, LOCAL), F32),
        pltpu.VMEM((LOCAL, LOCAL), BF16),
        pltpu.VMEM((LOCAL, LOCAL), BF16),
        pltpu.VMEM((LOCAL, LOCAL), BF16),
        pltpu.VMEM((LOCAL, LOCAL), BF16),
        pltpu.VMEM((LOCAL, LOCAL), BF16),
        pltpu.VMEM((LOCAL, LOCAL), BF16),
        pltpu.VMEM((ES, ES, big), F32),
        pltpu.VMEM((DH, DW, big), F32),
        pltpu.VMEM((5, ES, ES, LANES), F32),
        pltpu.VMEM((DH * DW, LANES), BF16),
        pltpu.VMEM((DH * DW, LANES), BF16),
        pltpu.VMEM((2, SUB, LOCAL), BF16),
        pltpu.VMEM((LOCAL, COLS), BF16),
        pltpu.VMEM((LOCAL, COLS), BF16),
        pltpu.VMEM((ES, ES, COLS), F32),
        pltpu.VMEM((CS, ES, COLS), F32),
        pltpu.VMEM((ES, ES, COLS), F32),
        pltpu.VMEM((DH, DW, COLS), F32),
        pltpu.VMEM((DH, DW, COLS), F32),
        pltpu.VMEM((ITERS, ES, ES, COLS), F32),
        pltpu.VMEM((2, LANES, N * W * SUB), BF16),
        pltpu.VMEM((N, W, R0, COLS), F32),
        pltpu.VMEM((ITERS, N, W, SUB, COLS), F32),
        pltpu.VMEM((2, H, ES, big), F32),
        pltpu.VMEM((2, H, ES, big), F32),
        pltpu.VMEM((2, H, ES, big), F32),
        pltpu.VMEM((4, H, SUB, big), F32),
        pltpu.VMEM((ITERS, 2, H, ES, COLS), F32),
        pltpu.VMEM((ITERS, 2, H, ES, COLS), F32),
        pltpu.VMEM((ITERS, 2, H, ES, COLS), F32),
        pltpu.VMEM((ITERS, 4, H, SUB, COLS), F32),
        pltpu.SemaphoreType.DMA((ITERS + 1, 8)),
        pltpu.SemaphoreType.DMA((ITERS + 1, 8)),
        pltpu.SemaphoreType.DMA((ITERS + 1, CHIPS)),
        pltpu.SemaphoreType.DMA((ITERS + 1, CHIPS)),
        pltpu.SemaphoreType.DMA((ITERS + 1, N // 2)),
        pltpu.SemaphoreType.DMA((ITERS + 1, N // 2)),
        pltpu.SemaphoreType.DMA,
        pltpu.SemaphoreType.DMA((4,)),
        pltpu.VMEM((LANES, LANES), F32),
        pltpu.VMEM((LANES, LOCAL), F32),
        pltpu.VMEM((2 * H * ES, LOCAL), BF16),
        pltpu.VMEM((2 * H * ES, LOCAL), BF16),
    ]
    out = jax.ShapeDtypeStruct((CS, ES, COLS), F32)
    anywhere = pl.BlockSpec(memory_space=pl.ANY)
    smem = pl.BlockSpec(memory_space=pltpu.SMEM)
    *fields, size = pl.pallas_call(
        functools.partial(kernel, (N, W, ES, OV, CS, COLS, MODES, KR)),
        out_shape=(out,) * 4 + (jax.ShapeDtypeStruct((SUB, COLS), F32),),
        in_specs=[vmem] * 3 + [smem, vmem, anywhere] + [vmem] * 2,
        out_specs=(anywhere,) * 4 + (vmem,),
        scratch_shapes=scratch,
        compiler_params=pltpu.CompilerParams(
            collective_id=0, has_side_effects=True, vmem_limit_bytes=67043328
        ),
        name="schwarz",
    )(
        right_side,
        initial_guess,
        class_map,
        class_conductivity,
        window_index[0],
        local_inverse[0, 0],
        coarse_basis,
        coarse_inverse,
    )
    block = CS // 4
    part = pl.BlockSpec((block, ES, COLS), lambda i: (i, 0, 0))
    done = pl.BlockSpec((block, CS, COLS), lambda i: (i, 0, 0))
    return pl.pallas_call(
        functools.partial(finish, OV, CS),
        grid=(CS // block,),
        out_shape=(jax.ShapeDtypeStruct(right_side.shape, F32),) * 2,
        in_specs=[part] * 4 + [pl.BlockSpec((SUB, COLS), lambda i: (0, 0))],
        out_specs=(done, done),
        name="finish",
    )(*fields, size)


def solution(mesh):
    in_specs = (
        P("narrow", "wide", None),
        P("narrow", "wide", None),
        P("narrow", "wide"),
        P(),
        P("narrow", "wide", None),
        P("narrow", "wide", None, None),
        P("narrow", "wide", None, None),
        P("wide", "narrow"),
    )
    out_specs = (P("narrow", "wide", None), P("narrow", "wide", None))
    body = functools.partial(local, mesh.shape["narrow"], mesh.shape["wide"])
    return jax.shard_map(body, mesh=mesh, in_specs=in_specs, out_specs=out_specs, check_vma=False)
```
